512 devices in a mesh: band: 8 (over y), rows: 64 (over x, z, core).
Axes of the slice: x: 4, y: 8, z: 8, core: 2. Of those that a mesh axis runs over, the one named last changes fastest.
Arguments:
- start_iterate: float32 [16384, 16, 128], P(('band', 'rows')), may hold values from 0 to 2
- right_side: float32 [16384, 16, 128], P(('band', 'rows')), as said below
- diag_table: float32 [8, 128, 128], replicated, as said below
- inverse_table: float32 [8, 128, 128], replicated, as said below
- coupling_tiles: float32 [8, 128, 128], replicated, may hold values from 0 to 0.009375
- diag_index: int32 [16384], P(('band', 'rows')), may hold values from 0 to 7
- tile_index: int32 [16384, 4], P(('band', 'rows')), may hold values from 0 to 7
- source_owner: int32 [16384, 2], P(('band', 'rows')), may hold values from 0 to 63, all different within a row; in each aligned block of 32 rows (0 to 31, 32 to 63, ...) at most 2 rows name the same one
- source_local: int32 [16384, 2], P(('band', 'rows')), may hold values from 0 to 31
- aggregate_map: int32 [16384, 1], P(('band', 'rows')), may hold values from 0 to 4095
Outputs:
- swept_iterate: float32 [16384, 16, 128], P(('band', 'rows'))
The draws below stay inside these ranges and needn't reach their ends.
Inputs may be any that keep to these rules, and one draw needn't show every extreme that they name: `source_owner`: within each aligned block of 32 rows (the rows of one device) no owner is named by more than 2 entries, a bound that some block reaches; the 2 owners of one row differ. `aggregate_map`: every aggregate is named by at least one block row. `diag_table`: diagonal entries lie from 6 to 10; off-diagonal entries are nonpositive with magnitude at most 5 / 128. `inverse_table`: entries are nonnegative; each block is a first-order approximation of the inverse of the diagonal block of the same index, not its exact inverse. `right_side`: entries are nonnegative.
All inputs are finite; a program needn't handle non-finite values.
Results may differ from the reference program's by a relative error of at most 0.0001.
Values sent between devices are 32-bit elements; how exact they have to be, the bound alone decides.
A program may use at most 64 MiB of HBM per device.

```python
import math
import jax
import jax.numpy as jnp
import numpy as np
from jax import lax

PH = 128
NV = 16
BR_DEV = 32
K = 2
NT = 8
ND = 8
CAP = 2
NB = 16384
NAGG = 4096
N_ROWS = 64


def diagonal_parts(key):
    first_key = jax.random.fold_in(key, 101)
    second_key = jax.random.fold_in(key, 202)
    spread = jax.random.uniform(first_key, (ND, PH), jnp.float32)
    rates = jax.random.uniform(second_key, (ND, PH, PH), jnp.float32)
    diagonal = 6.0 + 4.0 * spread
    rates = 5.0 / PH * rates
    identity = jnp.eye(PH, dtype=jnp.float32)
    rates = rates * (1.0 - identity)
    return (diagonal, rates, identity)


def draw_diag_table(key, part):
    diagonal, rates, identity = diagonal_parts(key)
    return diagonal[:, :, None] * identity - rates


def draw_inverse_table(key, part):
    diagonal, rates, identity = diagonal_parts(key)
    recip = 1.0 / diagonal
    return recip[:, :, None] * identity + rates * recip[:, :, None] * recip[:, None, :]


def draw_right_side(key, part):
    first_key = jax.random.fold_in(key, 303)
    second_key = jax.random.fold_in(key, 404)
    level = jax.random.uniform(first_key, (NB, 1, 1), jnp.float32)
    entries = jax.random.uniform(second_key, (NB, NV, PH), jnp.float32)
    scale = jnp.exp(jnp.log(0.3) + level * jnp.log(10.0))
    values = 2.0 * entries
    return scale * values


def touch_ends(values, stream_key, least, largest):
    extent = values.shape
    spot = [jax.random.randint(jax.random.fold_in(stream_key, axis), (), 0, extent[axis]) for axis in range(len(extent))]
    values = values.at[tuple(spot)].set(least)
    longest = extent.index(max(extent))
    spot[longest] = (spot[longest] + 1) % extent[longest]
    return values.at[tuple(spot)].set(largest)


def block_levels(rng, dims, cuts, smallest, top_value):
    def one(position, parts):
        draws = jax.random.uniform(jax.random.fold_in(jax.random.fold_in(rng, 6), position), (parts,), jnp.float32, smallest / len(cuts), top_value / len(cuts))
        return jnp.repeat(jnp.exp(draws), dims[position] // parts).reshape((-1,) + (1,) * (len(dims) - position - 1))

    loudness = one(*cuts[0])
    for cut in cuts[1:]:
        loudness = loudness * one(*cut)
    return loudness


def choose_distinct(stream_key, rows, amount, top, lift):
    order = jax.random.permutation(jax.random.fold_in(stream_key, 1), amount)
    boost = order
    for power in range(3):
        boost = boost * boost // amount
    boost = boost * lift // amount
    chance = jax.random.randint(jax.random.fold_in(stream_key, 2), (rows, amount), 0, 4096) + boost
    fixed_rows = jax.random.permutation(jax.random.fold_in(stream_key, 3), rows)[jnp.arange(amount) % rows]
    chance = jnp.where(jnp.arange(rows)[:, None] == fixed_rows[None, :], 1 << 14, chance)
    merit = chance * amount + jnp.arange(amount)
    return lax.top_k(merit.astype(jnp.int32), top)[1].astype(jnp.int32)


def shared_out(stream_key, own, number, rows, count, top, reach, lean):
    sequence = jax.random.permutation(stream_key, count)
    crowded, common = load_shares(count, rows * top, reach, lean, True), load_shares(count, rows * top, reach, lean, False)
    places = jnp.arange(count)

    def named(tallies, offset_by):
        used = int((tallies > 0).sum())
        fixed = max(1, used // 4)
        passed = fixed + (places - fixed + offset_by * (used - fixed)) % max(1, count - fixed)
        return jnp.zeros((count,), jnp.int32).at[sequence[jnp.where(places < fixed, places, passed)]].set(jnp.asarray(tallies, jnp.int32))

    tallies = jnp.where(number % 4 == 0, named(crowded, number // 4), named(common, number - number // 4 - 1))
    mixed = jax.random.permutation(jax.random.fold_in(own, 3), count)
    source_of, sink = mixed[0:count // 2 * 2:2], mixed[1:count // 2 * 2:2]
    margin = jnp.minimum(tallies[source_of] - 1, reach - tallies[sink]) // 2
    margin = jnp.where((source_of == sequence[0]) | (sink == sequence[0]) | (tallies[sink] == 0), 0, jnp.maximum(margin, 0))
    passed = jax.random.randint(jax.random.fold_in(own, 4), (count // 2,), 0, 1 << 20) % (margin + 1)
    tallies = tallies.at[source_of].add(-passed).at[sink].add(passed)
    labels = jnp.searchsorted(jnp.cumsum(tallies), jnp.arange(rows * top), side="right").astype(jnp.int32)
    table = labels.reshape(top, rows).T
    table = table[jax.random.permutation(jax.random.fold_in(own, 1), rows)]
    offset_by = jax.random.randint(jax.random.fold_in(own, 2), (rows, 1), 0, top)
    return jnp.take_along_axis(table, (jnp.arange(top)[None, :] + offset_by) % top, axis=1)


def load_shares(amount, total, limit, slope, full):
    weights = [(1 << 20) // math.isqrt(standing ** slope) + 1 for standing in range(1, amount + 1)]
    largest = limit if full else min(limit, max(-(-total // amount), total * weights[0] // sum(weights)))
    least = 1 if total - largest >= amount - 1 else 0
    holding, rest = [largest] + [least] * (amount - 1), total - largest - least * (amount - 1)
    while rest > 0:
        candidates = [i for i in range(1, amount) if holding[i] < largest] or [i for i in range(1, amount) if holding[i] < limit]
        whole, left = sum([weights[i] for i in candidates]), rest
        for i in candidates:
            extra = min(limit - holding[i], max(1, left * weights[i] // whole), rest)
            holding[i] = holding[i] + extra
            rest = rest - extra
    return np.array(holding)


def setup_inputs(seed: int = 0) -> dict:
    arg_keys = jax.random.split(jax.random.key(seed), 11)
    start_iterate = jnp.clip(2.0 * jax.random.uniform(arg_keys[0], (NB, NV, PH), jnp.float32) ** block_levels(arg_keys[0], (NB, NV, PH), ((0, 512),), -0.2, 0.2), 0.0, 2.0)
    right_side = draw_right_side(jax.random.fold_in(arg_keys[10], 71), 0)
    diag_table = draw_diag_table(jax.random.fold_in(arg_keys[10], 71), 0)
    inverse_table = draw_inverse_table(jax.random.fold_in(arg_keys[10], 71), 0)
    coupling_tiles = jnp.clip(jax.random.uniform(arg_keys[4], (NT, PH, PH), jnp.float32, 0.0, 0.009375), 0.0, 0.009375)
    diag_index = touch_ends(jax.random.randint(arg_keys[5], (NB,), 0, ND), jax.random.fold_in(arg_keys[5], 1), 0, ND - 1).astype(jnp.int32)
    tile_index = touch_ends(jax.random.randint(arg_keys[6], (NB, K + 2), 0, NT), jax.random.fold_in(arg_keys[6], 1), 0, NT - 1).astype(jnp.int32)
    source_owner_keys = jax.random.split(jax.random.fold_in(arg_keys[7], 1), NB // BR_DEV)
    source_owner_turns = jax.random.permutation(jax.random.fold_in(arg_keys[7], 3), NB // BR_DEV)
    source_owner = jax.vmap(lambda own, number: shared_out(jax.random.fold_in(arg_keys[7], 2), own, number, BR_DEV, N_ROWS, K, CAP, 2))(source_owner_keys, source_owner_turns).reshape((NB, K))
    source_local = touch_ends(jax.random.randint(arg_keys[8], (NB, K), 0, BR_DEV), jax.random.fold_in(arg_keys[8], 1), 0, BR_DEV - 1).astype(jnp.int32)
    aggregate_map = choose_distinct(arg_keys[9], NB, NAGG, 1, 0)
    return dict(start_iterate=start_iterate, right_side=right_side, diag_table=diag_table, inverse_table=inverse_table, coupling_tiles=coupling_tiles, diag_index=diag_index, tile_index=tile_index, source_owner=source_owner, source_local=source_local, aggregate_map=aggregate_map)


HIGH = lax.Precision.HIGHEST


def blockwise(handler, count, block_rows):
    starts = jnp.arange(count // block_rows, dtype=jnp.int32) * block_rows
    pieces = lax.map(handler, starts)
    return pieces.reshape((count,) + pieces.shape[2:])


def coupling(iterate, tile_index, source_owner, source_local, coupling_tiles):
    band_rows = BR_DEV * N_ROWS
    row_ids = jnp.arange(NB, dtype=jnp.int32)
    band_start = (row_ids // band_rows) * band_rows
    columns = (band_start[:, None] + source_owner * BR_DEV + source_local).astype(jnp.int32)
    padding = jnp.zeros((band_rows, NV, PH), jnp.float32)
    from_lower = jnp.concatenate([padding, iterate[: NB - band_rows]], axis=0)
    from_upper = jnp.concatenate([iterate[band_rows:], padding], axis=0)

    def one_block(start):
        picked = lax.dynamic_slice_in_dim(columns, start, BR_DEV, 0)
        remote = jnp.take(iterate, picked, axis=0)
        below = lax.dynamic_slice_in_dim(from_lower, start, BR_DEV, 0)
        above = lax.dynamic_slice_in_dim(from_upper, start, BR_DEV, 0)
        sources = jnp.concatenate([remote, below[:, None], above[:, None]], axis=1)
        chosen = jnp.take(coupling_tiles, lax.dynamic_slice_in_dim(tile_index, start, BR_DEV, 0), axis=0)
        return jnp.einsum("rkst,rkvt->rvs", chosen, sources, precision=HIGH)

    return blockwise(one_block, NB, BR_DEV)


def apply_table(table, index, iterate):
    def one_block(start):
        chosen = jnp.take(table, lax.dynamic_slice_in_dim(index, start, BR_DEV, 0), axis=0)
        part_rows = lax.dynamic_slice_in_dim(iterate, start, BR_DEV, 0)
        return jnp.einsum("rst,rvt->rvs", chosen, part_rows, precision=HIGH)

    return blockwise(one_block, NB, BR_DEV)


def reference(start_iterate, right_side, diag_table, inverse_table, coupling_tiles, diag_index, tile_index, source_owner, source_local, aggregate_map):
    iterate = start_iterate
    for sweep_pass in range(2):
        coupled = coupling(iterate, tile_index, source_owner, source_local, coupling_tiles)
        iterate = apply_table(inverse_table, diag_index, right_side + coupled)
    coupled = coupling(iterate, tile_index, source_owner, source_local, coupling_tiles)
    residual = right_side + coupled - apply_table(diag_table, diag_index, iterate)
    residual_sums = jnp.sum(residual, axis=2)
    table_sums = jnp.sum(diag_table, axis=(1, 2))
    block_sums = jnp.take(table_sums, diag_index)
    groups = aggregate_map[:, 0]
    coarse_residual = jax.ops.segment_sum(residual_sums, groups, num_segments=NAGG)
    coarse_diag = jax.ops.segment_sum(block_sums, groups, num_segments=NAGG)
    correction = coarse_residual / coarse_diag[:, None]
    return iterate + jnp.take(correction, groups, axis=0)[:, :, None]
```

```python
import functools
import jax
import jax.numpy as jnp
from jax import lax
from jax.experimental import pallas as pl
from jax.experimental.pallas import tpu as pltpu
from jax.sharding import PartitionSpec as P

MESH = pl.DeviceIdType.MESH
F32 = jnp.float32
BF16 = jnp.bfloat16
I32 = jnp.int32
PH = 128
NV = 16
NT = 8
CORES = 2
GRID_XZ = {64: (4, 8), 8: (2, 2)}


def iota(shape, dim):
    return lax.broadcasted_iota(I32, shape, dim)


def split(value):
    high = value.astype(BF16)
    return high, (value - high.astype(F32)).astype(BF16)


def nt_dot(a, b):
    return lax.dot_general(a, b, (((1,), (1,)), ((), ())), preferred_element_type=F32)


def dot(a, b):
    return jnp.dot(a, b, preferred_element_type=F32)


def kernel(
    n_band,
    n_rows,
    diag_s,
    tile_s,
    owner_s,
    local_s,
    agg_s,
    v_ref,
    rhs_ref,
    dtab,
    itab,
    ttab,
    out_ref,
    tst,
    ist,
    cols,
    colt,
    whl,
    xs,
    msg,
    recvreq,
    slots_v,
    reqs_s,
    slots_s,
    agg_row,
    meta_s,
    meta_t,
    match,
    bs_flat,
    res_flat,
    stage_a,
    stage_b,
    stage_m,
    stage_p,
    stage_o,
    send_big,
    arrived_one,
    arrived_two,
    low,
    up,
    first,
    xhl,
    send_small,
    recv_small,
    u_send,
    u_low,
    u_up,
    zbuf,
    req_sem,
    agg_sem,
    big_sem,
    band_sem,
    small_sem,
    uband_sem,
    a_sem,
    b_sem,
    loc_sem,
):
    arrived = (arrived_one, arrived_two)
    n_x, n_z = GRID_XZ[n_rows]
    n_zc = n_z * CORES
    n_xy = n_x * n_band
    block_rows = v_ref.shape[0]
    flat = block_rows * NV
    b = lax.axis_index("band")
    r = lax.axis_index("rows")
    x = r // n_zc
    zc = r % n_zc
    xy = x * n_band + b
    below = (b + n_band - 1) % n_band
    above = (b + 1) % n_band

    def zc_peer(step):
        return (b, x * n_zc + (zc + step) % n_zc)

    def xy_peer(step):
        peer = (xy + step) % n_xy
        return (peer % n_band, (peer // n_band) * n_zc + zc)

    barrier = pltpu.get_barrier_semaphore()

    def greet_rows(step, carry):
        pl.semaphore_signal(barrier, inc=1, device_id=(b, (r + step) % n_rows), device_id_type=MESH)
        return carry

    lax.fori_loop(1, n_rows, greet_rows, 0)

    def greet_planes(step, carry):
        py = (b + 1 + step // n_x) % n_band
        px = (x + step % n_x) % n_x
        pl.semaphore_signal(barrier, inc=1, device_id=(py, px * n_zc + zc), device_id_type=MESH)
        return carry

    lax.fori_loop(0, n_x * (n_band - 1), greet_planes, 0)

    sub = iota((n_rows, PH), 0)
    lane = iota((n_rows, PH), 1)
    lane1 = iota((1, PH), 1)
    parity = lane % 2
    is_local = (lane1 % 4) < 2
    lane_flat = iota((1, flat), 1) // NV

    def collect(i, carry):
        wants, count, slots, aggs, dflat, lowflat, upflat = carry
        for k in range(2):
            off = (r - owner_s[i, k] + n_rows) % n_rows
            hit = sub == off
            value = jnp.where(is_local, local_s[i, k], tile_s[i, k])
            wants = jnp.where(hit & (count == parity), value, wants)
            rank = jnp.sum(jnp.where(hit & (count > 0), 1, 0), axis=0, keepdims=True)
            slots = jnp.where(lane1 == 2 * i + k, off * 2 + jnp.clip(rank, 0, 1), slots)
            count = count + hit.astype(I32)
        here = lane_flat == i
        aggs = jnp.where(lane1 % block_rows == i, agg_s[i, 0], aggs)
        dflat = jnp.where(here, diag_s[i], dflat)
        lowflat = jnp.where(here, tile_s[i, 2], lowflat)
        upflat = jnp.where(here, tile_s[i, 3], upflat)
        return wants, count, slots, aggs, dflat, lowflat, upflat

    zero_rows = jnp.zeros((n_rows, PH), I32)
    zero_row = jnp.zeros((1, PH), I32)
    zero_flat = jnp.zeros((1, flat), I32)
    wants, _, slots, aggs, dflat, lowflat, upflat = lax.fori_loop(
        0, block_rows, collect, (zero_rows, zero_rows, zero_row, zero_row, zero_flat, zero_flat, zero_flat)
    )
    for off in range(n_rows):
        msg[off] = wants[off : off + 1, :]
    recvreq[0] = wants[0:1, :]
    slots_v[0] = slots
    agg_row[0] = aggs.astype(F32)
    meta_s[pl.ds(zc, 1)] = aggs.astype(F32)[None]
    meta_t[pl.ds(xy, 1)] = aggs.astype(F32)[None]
    slot_copy = pltpu.make_async_copy(slots_v, slots_s, loc_sem.at[0])
    slot_copy.start()

    col_t = jnp.concatenate([jnp.sum(ttab[t], axis=0, keepdims=True) for t in range(NT)], axis=0)
    col_d = jnp.concatenate([jnp.sum(dtab[t], axis=0, keepdims=True) for t in range(NT)], axis=0)
    for t in range(NT):
        colt[t] = col_t[t : t + 1, :]
    cols[...] = jnp.concatenate(split(col_t) + split(col_d), axis=0)
    table_sum = jnp.sum(col_d, axis=1, keepdims=True)
    sub8 = iota((NT, flat), 0)
    block_sum = jnp.sum(jnp.where(sub8 == dflat, table_sum, 0.0), axis=0, keepdims=True)
    for q in range(4):
        bs_flat[0, q : q + 1, :] = block_sum[:, q * PH : (q + 1) * PH]
    stage_a[0, pl.ds(zc, 1)] = bs_flat[...]

    pl.semaphore_wait(barrier, n_rows - 1 + n_x * (n_band - 1))

    def rows_copies(source, target, width, sems, step_sign):
        def copy(step):
            peer = (r + step_sign * step + n_rows) % n_rows
            return pltpu.make_async_remote_copy(
                src_ref=source(step),
                dst_ref=target.at[pl.ds(step * width, width)],
                send_sem=sems.at[0],
                recv_sem=sems.at[1],
                device_id=(b, peer),
                device_id_type=MESH,
            )

        def start(step, carry):
            copy(step).start()
            return carry

        lax.fori_loop(1, n_rows, start, 0)

    def drain(ref, count, sems):
        part = ref.at[pl.ds(0, count)]
        pltpu.make_async_copy(part, part, sems.at[0]).wait()

    def arrive(ref, count, sems):
        part = ref.at[pl.ds(0, count)]
        pltpu.make_async_copy(part, part, sems.at[1]).wait()

    def band_copies(source, to_above, to_below, sems):
        copies = []
        for side, (target, peer) in enumerate(((to_above, above), (to_below, below))):
            copy = pltpu.make_async_remote_copy(
                src_ref=source,
                dst_ref=target,
                send_sem=sems.at[side, 0],
                recv_sem=sems.at[side, 1],
                device_id=(peer, r),
                device_id_type=MESH,
            )
            copy.start()
            copies.append(copy)
        return copies

    rows_copies(lambda step: msg.at[pl.ds(step, 1)], recvreq, 1, req_sem, -1)

    def group_copies(source, target, index, peer_of, count, sems):
        def start(step, carry):
            pltpu.make_async_remote_copy(
                src_ref=source(step),
                dst_ref=target.at[pl.ds(index, 1)],
                send_sem=sems.at[0],
                recv_sem=sems.at[1],
                device_id=peer_of(step),
                device_id_type=MESH,
            ).start()
            return carry

        lax.fori_loop(1, count, start, 0)

    group_copies(lambda step: agg_row, meta_s, zc, zc_peer, n_zc, agg_sem.at[0])
    group_copies(lambda step: agg_row, meta_t, xy, xy_peer, n_xy, agg_sem.at[1])
    group_copies(lambda step: bs_flat, stage_a.at[0], zc, zc_peer, n_zc, a_sem.at[0])
    band1 = band_copies(v_ref, low.at[0], up.at[0], band_sem.at[0])

    def prepare(t, carry):
        rows = pl.ds(pl.multiple_of(t * PH, PH), PH)
        for source, target in ((ttab, tst), (itab, ist)):
            high, rest = split(jnp.transpose(source[t]))
            target[rows, 0:PH] = high
            target[rows, PH : 2 * PH] = rest
        return carry

    arrive(recvreq, n_rows - 1, req_sem)
    req_copy = pltpu.make_async_copy(recvreq, reqs_s, loc_sem.at[1])
    req_copy.start()
    slot_copy.wait()
    req_copy.wait()

    def send_blocks(source, which):
        def gather(off, carry):
            for rank in range(2):
                send_big[which, 2 * off + rank] = source[reqs_s[off, 0, rank]]
            return carry

        lax.fori_loop(0, n_rows, gather, 0)
        arrived[which][0:2] = send_big[which, 0:2]
        rows_copies(
            lambda step: send_big.at[which].at[pl.ds(2 * step, 2)],
            arrived[which],
            2,
            big_sem.at[which],
            1,
        )

    send_blocks(v_ref, 0)
    lax.fori_loop(0, NT, prepare, 0)

    def coupled_apply(which, target):
        def form(i, carry):
            rows = pl.ds(pl.multiple_of(i * NV, NV), NV)
            rest_rows = pl.ds(pl.multiple_of(flat + i * NV, NV), NV)
            sources = (
                arrived[which][slots_s[0, 0, 2 * i]],
                arrived[which][slots_s[0, 0, 2 * i + 1]],
                low[which, i],
                up[which, i],
            )
            tiles = (
                tile_s[i, 0],
                tile_s[i, 1],
                jnp.where(b == 0, -1, tile_s[i, 2]),
                jnp.where(b == n_band - 1, -1, tile_s[i, 3]),
            )
            for t in range(NT):
                total = jnp.where(tiles[0] == t, 1.0, 0.0) * sources[0]
                for k in range(1, 4):
                    total = total + jnp.where(tiles[k] == t, 1.0, 0.0) * sources[k]
                high, rest = split(total)
                whl[rows, t * PH : (t + 1) * PH] = high
                whl[rest_rows, t * PH : (t + 1) * PH] = rest
            return carry

        lax.fori_loop(0, block_rows, form, 0)
        y = dot(whl[...], tst[...])
        y = y[:flat] + y[flat:]
        xs[...] = rhs_ref[...].reshape(flat, PH) + (y[:, :PH] + y[:, PH:])

        def form_diag(i, carry):
            rows = pl.ds(pl.multiple_of(i * NV, NV), NV)
            rest_rows = pl.ds(pl.multiple_of(flat + i * NV, NV), NV)
            value = xs[rows, :]
            rest = value - value.astype(BF16).astype(F32)
            for t in range(NT):
                keep = jnp.where(diag_s[i] == t, 1.0, 0.0)
                whl[rows, t * PH : (t + 1) * PH] = (value * keep).astype(BF16)
                whl[rest_rows, t * PH : (t + 1) * PH] = (rest * keep).astype(BF16)
            return carry

        lax.fori_loop(0, block_rows, form_diag, 0)
        y = dot(whl[...], ist[...])
        y = y[:flat] + y[flat:]
        target[...] = (y[:, :PH] + y[:, PH:]).reshape(block_rows, NV, PH)

    arrive(meta_s, n_zc - 1, agg_sem.at[0])
    arrive(meta_t, n_xy - 1, agg_sem.at[1])
    lanes = iota((1, PH), 1)
    per_row = PH // block_rows
    pieces = []
    for group in range(n_zc // per_row):
        piece = jnp.zeros((1, PH), F32)
        for place in range(per_row):
            piece = jnp.where(lanes // block_rows == place, meta_s[group * per_row + place], piece)
        pieces.append(piece)
    source_row = jnp.concatenate(pieces, axis=1)
    own_lane = iota((block_rows, PH), 1) == iota((block_rows, PH), 0)

    def build(d, carry):
        column = jnp.sum(jnp.where(own_lane, meta_t[d], 0.0), axis=1, keepdims=True)
        rows = pl.ds(pl.multiple_of(d * block_rows, block_rows), block_rows)
        match[rows, :] = jnp.where(column == source_row, 1.0, 0.0).astype(BF16)
        return carry

    lax.fori_loop(0, n_xy, build, 0)
    block_lane = (iota((8, PH), 1) // NV) == iota((8, PH), 0)
    fold = jnp.where(iota((PH, PH), 0) % NV == iota((PH, PH), 1) % NV, 1.0, 0.0).astype(BF16)

    def fold_lanes(value):
        high, rest = split(value)
        return dot(high, fold) + dot(rest, fold)

    def to_flat_rows(value, q):
        picked = jnp.where(block_lane, value[q * 8 : (q + 1) * 8, :], 0.0)
        return jnp.sum(picked, axis=0, keepdims=True)

    def partial_sums(which):
        arrive(stage_a.at[which], n_zc - 1, a_sem.at[which])

        def spread(source, carry):
            value = stage_a[which, source]
            for q in range(4):
                rows = pl.ds(pl.multiple_of(source * block_rows + q * 8, 8), 8)
                stage_m[rows, :] = jnp.where(block_lane, value[q : q + 1, :], 0.0)
            return carry

        lax.fori_loop(0, n_zc, spread, 0)
        both = jnp.concatenate(split(stage_m[...]), axis=1)
        y = dot(match[...], both)
        stage_p[...] = fold_lanes(y[:, :PH] + y[:, PH:])

        def flatten(d, carry):
            value = stage_p[pl.ds(pl.multiple_of(d * block_rows, block_rows), block_rows), :]
            for q in range(4):
                stage_o[which, d, q : q + 1, :] = to_flat_rows(value, q)
            return carry

        lax.fori_loop(0, n_xy, flatten, 0)
        stage_b[which, pl.ds(xy, 1)] = stage_o[which, pl.ds(xy, 1)]

        def out_part(step):
            return stage_o.at[which].at[pl.ds((xy + step) % n_xy, 1)]

        group_copies(out_part, stage_b.at[which], xy, xy_peer, n_xy, b_sem.at[which])

    partial_sums(0)

    arrive(arrived[0], 2 * (n_rows - 1), big_sem.at[0])
    for copy in band1:
        copy.wait_recv()
    coupled_apply(0, first)
    send_blocks(first, 1)
    band2 = band_copies(first, low.at[1], up.at[1], band_sem.at[1])
    ones = jnp.ones((8, PH), BF16)
    rhs_parts = split(rhs_ref[...].reshape(flat, PH))
    rhs_sum = (nt_dot(ones, rhs_parts[0]) + nt_dot(ones, rhs_parts[1]))[0:1, :]
    arrive(arrived[1], 2 * (n_rows - 1), big_sem.at[1])
    for copy in band2:
        copy.wait_recv()
    coupled_apply(1, out_ref)

    second_parts = split(out_ref[...].reshape(flat, PH))
    projected = nt_dot(cols[...], second_parts[0]) + nt_dot(cols[...], second_parts[1])
    u_send[...] = projected[0:8] + projected[8:16]
    uband = band_copies(u_send, u_low, u_up, uband_sem)

    def edge(off, carry):
        for rank in range(2):
            value = out_ref[reqs_s[off, 0, rank]] * colt[reqs_s[off, 0, 2 + rank]]
            high, rest = split(value)
            place = pl.ds(pl.multiple_of((2 * off + rank) * NV, NV), NV)
            xhl[0, place, :] = high
            xhl[1, place, :] = rest
        return carry

    lax.fori_loop(0, n_rows, edge, 0)
    edges = nt_dot(ones, xhl[0]) + nt_dot(ones, xhl[1])
    for group in range(n_rows // 4):
        send_small[group] = edges[0:1, group * PH : (group + 1) * PH]
    recv_small[0] = edges[0:1, 0:PH]
    rows_copies(lambda step: send_small.at[pl.ds(step // 4, 1)], recv_small, 1, small_sem, 1)

    own = projected[16:24] + projected[24:32]
    local_sum = rhs_sum - jnp.sum(jnp.where(sub8 == dflat, own, 0.0), axis=0, keepdims=True)
    for copy in uband:
        copy.wait_recv()
    has_low = jnp.where(b == 0, 0.0, 1.0)
    has_up = jnp.where(b == n_band - 1, 0.0, 1.0)
    local_sum = local_sum + has_low * jnp.sum(
        jnp.where(sub8 == lowflat, u_low[...], 0.0), axis=0, keepdims=True
    )
    local_sum = local_sum + has_up * jnp.sum(
        jnp.where(sub8 == upflat, u_up[...], 0.0), axis=0, keepdims=True
    )
    arrive(recv_small, n_rows - 1, small_sem)

    def collect_edges(i, carry):
        total = jnp.zeros((1, PH), F32)
        for k in range(2):
            slot = slots_s[0, 0, 2 * i + k]
            piece = recv_small[slot // 2]
            total = total + jnp.where(lanes // NV == slot % 8, piece, 0.0)
        zbuf[i] = total
        return carry

    lax.fori_loop(0, block_rows, collect_edges, 0)
    rows_of = fold_lanes(zbuf[...].reshape(block_rows, PH))
    for q in range(4):
        res_flat[0, q : q + 1, :] = local_sum[:, q * PH : (q + 1) * PH] + to_flat_rows(rows_of, q)
    stage_a[1, pl.ds(zc, 1)] = res_flat[...]
    group_copies(lambda step: res_flat, stage_a.at[1], zc, zc_peer, n_zc, a_sem.at[1])
    partial_sums(1)

    arrive(stage_b.at[0], n_xy - 1, b_sem.at[0])
    denominator = jnp.sum(stage_b[0], axis=0)
    arrive(stage_b.at[1], n_xy - 1, b_sem.at[1])
    correction = jnp.sum(stage_b[1], axis=0) / denominator
    eye = iota((PH, PH), 0) == iota((PH, PH), 1)
    for q in range(4):
        column = jnp.sum(jnp.where(eye, correction[q : q + 1, :], 0.0), axis=1, keepdims=True)
        out_ref[q * 8 : (q + 1) * 8] = out_ref[q * 8 : (q + 1) * 8] + column.reshape(8, NV, 1)

    drain(msg, n_rows - 1, req_sem)
    drain(meta_s, n_zc - 1, agg_sem.at[0])
    drain(meta_t, n_xy - 1, agg_sem.at[1])
    for which in range(2):
        drain(send_big.at[which], 2 * (n_rows - 1), big_sem.at[which])
        drain(stage_a.at[which], n_zc - 1, a_sem.at[which])
        drain(stage_o.at[which], n_xy - 1, b_sem.at[which])
    drain(recv_small, n_rows - 1, small_sem)
    for copy in band1 + band2 + uband:
        copy.wait_send()


def on_device(
    start_iterate,
    right_side,
    diag_table,
    inverse_table,
    coupling_tiles,
    diag_index,
    tile_index,
    source_owner,
    source_local,
    aggregate_map,
):
    n_band = lax.axis_size("band")
    n_rows = lax.axis_size("rows")
    block_rows = start_iterate.shape[0]
    n_x, n_z = GRID_XZ[n_rows]
    n_zc, n_xy = n_z * CORES, n_x * n_band
    flat = block_rows * NV
    vmem = pltpu.VMEM
    dma = pltpu.SemaphoreType.DMA
    smem = pl.BlockSpec(memory_space=pltpu.SMEM)
    full = pl.BlockSpec(memory_space=pltpu.VMEM)
    scratch = [
        vmem((NT * PH, 2 * PH), BF16),
        vmem((NT * PH, 2 * PH), BF16),
        vmem((4 * NT, PH), BF16),
        vmem((NT, 1, PH), F32),
        vmem((2 * flat, NT * PH), BF16),
        vmem((flat, PH), F32),
        vmem((n_rows, 1, PH), I32),
        vmem((n_rows, 1, PH), I32),
        vmem((1, 1, PH), I32),
        pltpu.SMEM((n_rows, 1, PH), I32),
        pltpu.SMEM((1, 1, PH), I32),
        vmem((1, 1, PH), F32),
        vmem((n_zc, 1, PH), F32),
        vmem((n_xy, 1, PH), F32),
        vmem((n_xy * block_rows, n_zc * block_rows), BF16),
        vmem((1, 4, PH), F32),
        vmem((1, 4, PH), F32),
        vmem((2, n_zc, 4, PH), F32),
        vmem((2, n_xy, 4, PH), F32),
        vmem((n_zc * block_rows, PH), F32),
        vmem((n_xy * block_rows, PH), F32),
        vmem((2, n_xy, 4, PH), F32),
        vmem((2, 2 * n_rows, NV, PH), F32),
        vmem((2 * n_rows, NV, PH), F32),
        vmem((2 * n_rows, NV, PH), F32),
        vmem((2, block_rows, NV, PH), F32),
        vmem((2, block_rows, NV, PH), F32),
        vmem((block_rows, NV, PH), F32),
        vmem((2, 2 * n_rows * NV, PH), BF16),
        vmem((n_rows // 4, 1, PH), F32),
        vmem((n_rows, 1, PH), F32),
        vmem((NT, flat), F32),
        vmem((NT, flat), F32),
        vmem((NT, flat), F32),
        vmem((block_rows, 1, PH), F32),
        dma((2,)),
        dma((2, 2)),
        dma((2, 2)),
        dma((2, 2, 2)),
        dma((2,)),
        dma((2, 2)),
        dma((2, 2)),
        dma((2, 2)),
        dma((2,)),
    ]
    return pl.pallas_call(
        functools.partial(kernel, n_band, n_rows),
        out_shape=jax.ShapeDtypeStruct(start_iterate.shape, F32),
        in_specs=[smem] * 5 + [full] * 5,
        out_specs=full,
        scratch_shapes=scratch,
        compiler_params=pltpu.CompilerParams(
            collective_id=0, has_side_effects=True, vmem_limit_bytes=48 * 1024 * 1024
        ),
    )(
        diag_index,
        tile_index,
        source_owner,
        source_local,
        aggregate_map,
        start_iterate,
        right_side,
        diag_table,
        inverse_table,
        coupling_tiles,
    )


def solution(mesh):
    in_specs = (
        P(("band", "rows"), None, None),
        P(("band", "rows"), None, None),
        P(),
        P(),
        P(),
        P(("band", "rows")),
        P(("band", "rows"), None),
        P(("band", "rows"), None),
        P(("band", "rows"), None),
        P(("band", "rows"), None),
    )
    out_specs = P(("band", "rows"), None, None)
    return jax.shard_map(
        on_device, mesh=mesh, in_specs=in_specs, out_specs=out_specs, check_vma=False
    )
```

```python
import functools
import jax
import jax.numpy as jnp
from jax import lax
from jax.experimental import pallas as pl
from jax.experimental.pallas import tpu as pltpu
from jax.sharding import PartitionSpec as P

MESH = pl.DeviceIdType.MESH
F32 = jnp.float32
BF16 = jnp.bfloat16
I32 = jnp.int32
PH = 128
NV = 16
HALF = 8
PARTS = NV // HALF
NT = 8
CORES = 2
GRID_XZ = {64: (4, 8), 8: (2, 2)}


def iota(shape, dim):
    return lax.broadcasted_iota(I32, shape, dim)


def best(trips):
    return max(n for n in range(1, 10) if trips % n == 0)


def split(value):
    high = value.astype(BF16)
    return high, (value - high.astype(F32)).astype(BF16)


def nt_dot(a, b):
    return lax.dot_general(a, b, (((1,), (1,)), ((), ())), preferred_element_type=F32)


def dot(a, b):
    return jnp.dot(a, b, preferred_element_type=F32)


def kernel(
    n_band,
    n_rows,
    diag_s,
    tile_s,
    owner_s,
    local_s,
    agg_s,
    v_hbm,
    rhs_hbm,
    dtab_hbm,
    itab_hbm,
    ttab_hbm,
    out_ref,
    rhs_ref,
    dtab,
    itab,
    ttab,
    in_sem,
    tst,
    ist,
    cols,
    colt,
    whl,
    xs,
    msg,
    recvreq,
    slots_v,
    reqs_s,
    slots_s,
    agg_row,
    meta_s,
    meta_t,
    match,
    bs_flat,
    res_flat,
    stage_a,
    stage_b,
    stage_m,
    stage_p,
    stage_o,
    send_big,
    arrived_00,
    arrived_01,
    arrived_10,
    arrived_11,
    low,
    up,
    field_00,
    field_01,
    field_10,
    field_11,
    xhl,
    send_small,
    recv_small,
    u_send,
    u_low,
    u_up,
    zbuf,
    req_sem,
    agg_sem,
    big_sem,
    band_sem,
    small_sem,
    uband_sem,
    a_sem,
    b_sem,
    loc_sem,
):
    arrived = ((arrived_00, arrived_01), (arrived_10, arrived_11))
    field = ((field_00, field_01), (field_10, field_11))
    n_x, n_z = GRID_XZ[n_rows]
    n_zc = n_z * CORES
    n_xy = n_x * n_band
    block_rows = v_hbm.shape[0]
    flat = block_rows * NV
    b = lax.axis_index("band")
    r = lax.axis_index("rows")
    x = r // n_zc
    zc = r % n_zc
    xy = x * n_band + b
    below = (b + n_band - 1) % n_band
    above = (b + 1) % n_band

    def zc_peer(step):
        return (b, x * n_zc + lax.rem(zc + step, n_zc))

    def xy_peer(step):
        peer = lax.rem(xy + step, n_xy)
        return (lax.rem(peer, n_band), lax.div(peer, n_band) * n_zc + zc)

    loads = [
        pltpu.make_async_copy(source, target, in_sem.at[n])
        for n, (source, target) in enumerate(
            (
                (v_hbm.at[:, 0:HALF, :], field_00),
                (v_hbm.at[:, HALF:NV, :], field_01),
                (ttab_hbm, ttab),
                (dtab_hbm, dtab),
                (itab_hbm, itab),
                (rhs_hbm, rhs_ref),
            )
        )
    ]
    for load in loads:
        load.start()

    barrier = pltpu.get_barrier_semaphore()

    def greet_rows(step, carry):
        pl.semaphore_signal(barrier, inc=1, device_id=(b, lax.rem(r + step, n_rows)), device_id_type=MESH)
        return carry

    lax.fori_loop(1, n_rows, greet_rows, 0, unroll=best(n_rows - 1))

    def greet_planes(step, carry):
        py = lax.rem(b + 1 + lax.div(step, n_x), n_band)
        px = lax.rem(x + step, n_x)
        pl.semaphore_signal(barrier, inc=1, device_id=(py, px * n_zc + zc), device_id_type=MESH)
        return carry

    lax.fori_loop(0, n_x * (n_band - 1), greet_planes, 0, unroll=best(n_x * (n_band - 1)))

    sub = iota((n_rows, PH), 0)
    lane = iota((n_rows, PH), 1)
    lane1 = iota((1, PH), 1)
    parity = lane % 2
    is_local = (lane1 % 4) < 2
    lane_flat = iota((1, flat), 1) // NV

    def collect(i, carry):
        wants, count, slots, aggs, dflat, lowflat, upflat = carry
        for k in range(2):
            off = lax.rem(r - owner_s[k, i] + n_rows, n_rows)
            hit = sub == off
            value = jnp.where(is_local, local_s[k, i], tile_s[k, i])
            wants = jnp.where(hit & (count == parity), value, wants)
            rank = jnp.sum(jnp.where(hit & (count > 0), 1, 0), axis=0, keepdims=True)
            slots = jnp.where(lane1 == 2 * i + k, off * 2 + jnp.clip(rank, 0, 1), slots)
            count = count + hit.astype(I32)
        here = lane_flat == i
        aggs = jnp.where(lane1 % block_rows == i, agg_s[0, i], aggs)
        dflat = jnp.where(here, diag_s[i], dflat)
        lowflat = jnp.where(here, tile_s[2, i], lowflat)
        upflat = jnp.where(here, tile_s[3, i], upflat)
        return wants, count, slots, aggs, dflat, lowflat, upflat

    zero_rows = jnp.zeros((n_rows, PH), I32)
    zero_row = jnp.zeros((1, PH), I32)
    zero_flat = jnp.zeros((1, flat), I32)
    wants, _, slots, aggs, dflat, lowflat, upflat = lax.fori_loop(
        0, block_rows, collect, (zero_rows, zero_rows, zero_row, zero_row, zero_flat, zero_flat, zero_flat)
    )
    for off in range(n_rows):
        msg[off] = wants[off : off + 1, :]
    recvreq[0] = wants[0:1, :]
    slots_v[0] = slots
    agg_row[0] = aggs.astype(F32)
    meta_s[pl.ds(zc, 1)] = aggs.astype(F32)[None]
    meta_t[pl.ds(xy, 1)] = aggs.astype(F32)[None]
    slot_copy = pltpu.make_async_copy(slots_v, slots_s, loc_sem.at[0])
    slot_copy.start()

    for load in loads[:4]:
        load.wait()
    col_t = jnp.concatenate([jnp.sum(ttab[t], axis=0, keepdims=True) for t in range(NT)], axis=0)
    col_d = jnp.concatenate([jnp.sum(dtab[t], axis=0, keepdims=True) for t in range(NT)], axis=0)
    for t in range(NT):
        colt[t] = col_t[t : t + 1, :]
    cols[...] = jnp.concatenate(split(col_t) + split(col_d), axis=0)
    table_sum = jnp.sum(col_d, axis=1, keepdims=True)
    sub8 = iota((NT, flat), 0)
    block_sum = jnp.sum(jnp.where(sub8 == dflat, table_sum, 0.0), axis=0, keepdims=True)
    for q in range(4):
        bs_flat[0, q : q + 1, :] = block_sum[:, q * PH : (q + 1) * PH]
    stage_a[0, pl.ds(zc, 1)] = bs_flat[...]

    pl.semaphore_wait(barrier, n_rows - 1 + n_x * (n_band - 1))

    def rows_copies(source, target, width, sems, step_sign):
        def copy(step):
            peer = lax.rem(r + step_sign * step + n_rows, n_rows)
            return pltpu.make_async_remote_copy(
                src_ref=source(step),
                dst_ref=target.at[pl.ds(step * width, width)],
                send_sem=sems.at[0],
                recv_sem=sems.at[1],
                device_id=(b, peer),
                device_id_type=MESH,
            )

        def start(step, carry):
            copy(step).start()
            return carry

        lax.fori_loop(1, n_rows, start, 0, unroll=best(n_rows - 1))

    def drain(ref, count, sems):
        part = ref.at[pl.ds(0, count)]
        pltpu.make_async_copy(part, part, sems.at[0]).wait()

    def arrive(ref, count, sems):
        part = ref.at[pl.ds(0, count)]
        pltpu.make_async_copy(part, part, sems.at[1]).wait()

    def band_copies(source, to_above, to_below, sems):
        copies = []
        for side, (target, peer) in enumerate(((to_above, above), (to_below, below))):
            copy = pltpu.make_async_remote_copy(
                src_ref=source,
                dst_ref=target,
                send_sem=sems.at[side, 0],
                recv_sem=sems.at[side, 1],
                device_id=(peer, r),
                device_id_type=MESH,
            )
            copy.start()
            copies.append(copy)
        return copies

    rows_copies(lambda step: msg.at[pl.ds(step, 1)], recvreq, 1, req_sem, -1)

    def group_copies(source, target, index, peer_of, count, sems):
        def start(step, carry):
            pltpu.make_async_remote_copy(
                src_ref=source(step),
                dst_ref=target.at[pl.ds(index, 1)],
                send_sem=sems.at[0],
                recv_sem=sems.at[1],
                device_id=peer_of(step),
                device_id_type=MESH,
            ).start()
            return carry

        lax.fori_loop(1, count, start, 0, unroll=best(count - 1))

    group_copies(lambda step: agg_row, meta_s, zc, zc_peer, n_zc, agg_sem.at[0])
    group_copies(lambda step: agg_row, meta_t, xy, xy_peer, n_xy, agg_sem.at[1])
    group_copies(lambda step: bs_flat, stage_a.at[0], zc, zc_peer, n_zc, a_sem.at[0])

    def share_band(which, part):
        return band_copies(
            field[which][part],
            low.at[which].at[part],
            up.at[which].at[part],
            band_sem.at[which].at[part],
        )

    bands = [[share_band(0, part) for part in range(PARTS)], []]

    def prepare(t, carry):
        rows = pl.ds(pl.multiple_of(t * PH, PH), PH)
        for source, target in ((ttab, tst), (itab, ist)):
            high, rest = split(jnp.transpose(source[t]))
            target[rows, 0:PH] = high
            target[rows, PH : 2 * PH] = rest
        return carry

    arrive(recvreq, n_rows - 1, req_sem)
    req_copy = pltpu.make_async_copy(recvreq, reqs_s, loc_sem.at[1])
    req_copy.start()
    slot_copy.wait()
    req_copy.wait()

    def send_blocks(which, part):
        source = field[which][part]
        buffer = send_big.at[which].at[part]

        def gather(off, carry):
            for rank in range(2):
                buffer[2 * off + rank] = source[reqs_s[off, 0, rank]]
            return carry

        lax.fori_loop(0, n_rows, gather, 0, unroll=4)
        arrived[which][part][0:2] = buffer[0:2]
        rows_copies(
            lambda step: buffer.at[pl.ds(2 * step, 2)],
            arrived[which][part],
            2,
            big_sem.at[which].at[part],
            1,
        )

    for part in range(PARTS):
        send_blocks(0, part)
    for load in loads[4:]:
        load.wait()
    lax.fori_loop(0, NT, prepare, 0)
    size = block_rows * HALF

    def coupled_apply(which, part, target):
        arrive(arrived[which][part], 2 * (n_rows - 1), big_sem.at[which].at[part])
        for copy in bands[which][part]:
            copy.wait_recv()
        columns = slice(part * HALF, (part + 1) * HALF)

        def form(pair, carry):
            rows = pl.ds(pl.multiple_of(pair * NV, NV), NV)
            rest_rows = pl.ds(pl.multiple_of(size + pair * NV, NV), NV)
            sums = []
            for i in (2 * pair, 2 * pair + 1):
                sources = (
                    arrived[which][part][slots_s[0, 0, 2 * i]],
                    arrived[which][part][slots_s[0, 0, 2 * i + 1]],
                    low[which, part, i],
                    up[which, part, i],
                )
                tiles = (
                    tile_s[0, i],
                    tile_s[1, i],
                    jnp.where(b == 0, -1, tile_s[2, i]),
                    jnp.where(b == n_band - 1, -1, tile_s[3, i]),
                )
                totals = []
                for t in range(NT):
                    total = jnp.where(tiles[0] == t, 1.0, 0.0) * sources[0]
                    for k in range(1, 4):
                        total = total + jnp.where(tiles[k] == t, 1.0, 0.0) * sources[k]
                    totals.append(total)
                sums.append(totals)
            for t in range(NT):
                high, rest = split(jnp.concatenate([sums[0][t], sums[1][t]], axis=0))
                whl[rows, t * PH : (t + 1) * PH] = high
                whl[rest_rows, t * PH : (t + 1) * PH] = rest
            return carry

        lax.fori_loop(0, block_rows // 2, form, 0)
        y = dot(whl[...], tst[...])
        y = y[:size] + y[size:]
        xs[...] = rhs_ref[:, columns, :].reshape(size, PH) + (y[:, :PH] + y[:, PH:])

        def form_diag(pair, carry):
            rows = pl.ds(pl.multiple_of(pair * NV, NV), NV)
            rest_rows = pl.ds(pl.multiple_of(size + pair * NV, NV), NV)
            value = xs[rows, :]
            rest = value - value.astype(BF16).astype(F32)
            for t in range(NT):
                keep = [jnp.where(diag_s[2 * pair + n] == t, 1.0, 0.0) for n in range(2)]
                for source, place in ((value, rows), (rest, rest_rows)):
                    kept = jnp.concatenate(
                        [source[:HALF] * keep[0], source[HALF:] * keep[1]], axis=0
                    )
                    whl[place, t * PH : (t + 1) * PH] = kept.astype(BF16)
            return carry

        lax.fori_loop(0, block_rows // 2, form_diag, 0)
        y = dot(whl[...], ist[...])
        y = y[:size] + y[size:]
        target[...] = (y[:, :PH] + y[:, PH:]).reshape(block_rows, HALF, PH)

    arrive(meta_s, n_zc - 1, agg_sem.at[0])
    arrive(meta_t, n_xy - 1, agg_sem.at[1])
    lanes = iota((1, PH), 1)
    per_row = PH // block_rows
    pieces = []
    for group in range(n_zc // per_row):
        piece = jnp.zeros((1, PH), F32)
        for place in range(per_row):
            piece = jnp.where(lanes // block_rows == place, meta_s[group * per_row + place], piece)
        pieces.append(piece)
    source_row = jnp.concatenate(pieces, axis=1)
    own_lane = iota((block_rows, PH), 1) == iota((block_rows, PH), 0)

    def build(d, carry):
        column = jnp.sum(jnp.where(own_lane, meta_t[d], 0.0), axis=1, keepdims=True)
        rows = pl.ds(pl.multiple_of(d * block_rows, block_rows), block_rows)
        match[rows, :] = jnp.where(column == source_row, 1.0, 0.0).astype(BF16)
        return carry

    lax.fori_loop(0, n_xy, build, 0, unroll=2)
    block_lane = (iota((8, PH), 1) // NV) == iota((8, PH), 0)
    fold = jnp.where(iota((PH, PH), 0) % NV == iota((PH, PH), 1) % NV, 1.0, 0.0).astype(BF16)

    def fold_lanes(value):
        high, rest = split(value)
        return dot(high, fold) + dot(rest, fold)

    def to_flat_rows(value, q):
        picked = jnp.where(block_lane, value[q * 8 : (q + 1) * 8, :], 0.0)
        return jnp.sum(picked, axis=0, keepdims=True)

    def partial_sums(which):
        arrive(stage_a.at[which], n_zc - 1, a_sem.at[which])

        def spread(source, carry):
            value = stage_a[which, source]
            for q in range(4):
                rows = pl.ds(pl.multiple_of(source * block_rows + q * 8, 8), 8)
                stage_m[rows, :] = jnp.where(block_lane, value[q : q + 1, :], 0.0)
            return carry

        lax.fori_loop(0, n_zc, spread, 0, unroll=4)
        both = jnp.concatenate(split(stage_m[...]), axis=1)
        y = dot(match[...], both)
        stage_p[...] = fold_lanes(y[:, :PH] + y[:, PH:])

        def flatten(d, carry):
            value = stage_p[pl.ds(pl.multiple_of(d * block_rows, block_rows), block_rows), :]
            for q in range(4):
                stage_o[which, d, q : q + 1, :] = to_flat_rows(value, q)
            return carry

        lax.fori_loop(0, n_xy, flatten, 0, unroll=4)
        stage_b[which, pl.ds(xy, 1)] = stage_o[which, pl.ds(xy, 1)]

        def out_part(step):
            return stage_o.at[which].at[pl.ds(lax.rem(xy + step, n_xy), 1)]

        group_copies(out_part, stage_b.at[which], xy, xy_peer, n_xy, b_sem.at[which])

    partial_sums(0)

    for part in range(PARTS):
        coupled_apply(0, part, field[1][part])
        send_blocks(1, part)
        bands[1].append(share_band(1, part))
    ones = jnp.ones((8, PH), BF16)
    rhs_parts = split(rhs_ref[...].reshape(flat, PH))
    rhs_sum = (nt_dot(ones, rhs_parts[0]) + nt_dot(ones, rhs_parts[1]))[0:1, :]
    for part in range(PARTS):
        coupled_apply(1, part, out_ref.at[:, part * HALF : (part + 1) * HALF, :])

    second_parts = split(out_ref[...].reshape(flat, PH))
    projected = nt_dot(cols[...], second_parts[0]) + nt_dot(cols[...], second_parts[1])
    u_send[...] = projected[0:8] + projected[8:16]
    uband = band_copies(u_send, u_low, u_up, uband_sem)

    def edge(off, carry):
        for rank in range(2):
            value = out_ref[reqs_s[off, 0, rank]] * colt[reqs_s[off, 0, 2 + rank]]
            high, rest = split(value)
            place = pl.ds(pl.multiple_of((2 * off + rank) * NV, NV), NV)
            xhl[0, place, :] = high
            xhl[1, place, :] = rest
        return carry

    lax.fori_loop(0, n_rows, edge, 0, unroll=4)
    edges = nt_dot(ones, xhl[0]) + nt_dot(ones, xhl[1])
    for group in range(n_rows // 4):
        send_small[group] = edges[0:1, group * PH : (group + 1) * PH]
    recv_small[0] = edges[0:1, 0:PH]
    rows_copies(lambda step: send_small.at[pl.ds(lax.div(step, 4), 1)], recv_small, 1, small_sem, 1)

    own = projected[16:24] + projected[24:32]
    local_sum = rhs_sum - jnp.sum(jnp.where(sub8 == dflat, own, 0.0), axis=0, keepdims=True)
    for copy in uband:
        copy.wait_recv()
    has_low = jnp.where(b == 0, 0.0, 1.0)
    has_up = jnp.where(b == n_band - 1, 0.0, 1.0)
    local_sum = local_sum + has_low * jnp.sum(
        jnp.where(sub8 == lowflat, u_low[...], 0.0), axis=0, keepdims=True
    )
    local_sum = local_sum + has_up * jnp.sum(
        jnp.where(sub8 == upflat, u_up[...], 0.0), axis=0, keepdims=True
    )
    arrive(recv_small, n_rows - 1, small_sem)

    def collect_edges(i, carry):
        total = jnp.zeros((1, PH), F32)
        for k in range(2):
            slot = slots_s[0, 0, 2 * i + k]
            piece = recv_small[slot // 2]
            total = total + jnp.where(lanes // NV == slot % 8, piece, 0.0)
        zbuf[i] = total
        return carry

    lax.fori_loop(0, block_rows, collect_edges, 0, unroll=4)
    rows_of = fold_lanes(zbuf[...].reshape(block_rows, PH))
    for q in range(4):
        res_flat[0, q : q + 1, :] = local_sum[:, q * PH : (q + 1) * PH] + to_flat_rows(rows_of, q)
    stage_a[1, pl.ds(zc, 1)] = res_flat[...]
    group_copies(lambda step: res_flat, stage_a.at[1], zc, zc_peer, n_zc, a_sem.at[1])
    partial_sums(1)

    arrive(stage_b.at[0], n_xy - 1, b_sem.at[0])
    denominator = jnp.sum(stage_b[0], axis=0)
    arrive(stage_b.at[1], n_xy - 1, b_sem.at[1])
    correction = jnp.sum(stage_b[1], axis=0) / denominator
    eye = iota((PH, PH), 0) == iota((PH, PH), 1)
    for q in range(4):
        column = jnp.sum(jnp.where(eye, correction[q : q + 1, :], 0.0), axis=1, keepdims=True)
        out_ref[q * 8 : (q + 1) * 8] = out_ref[q * 8 : (q + 1) * 8] + column.reshape(8, NV, 1)

    drain(msg, n_rows - 1, req_sem)
    drain(meta_s, n_zc - 1, agg_sem.at[0])
    drain(meta_t, n_xy - 1, agg_sem.at[1])
    for which in range(2):
        for part in range(PARTS):
            drain(send_big.at[which].at[part], 2 * (n_rows - 1), big_sem.at[which].at[part])
            for copy in bands[which][part]:
                copy.wait_send()
        drain(stage_a.at[which], n_zc - 1, a_sem.at[which])
        drain(stage_o.at[which], n_xy - 1, b_sem.at[which])
    drain(recv_small, n_rows - 1, small_sem)
    for copy in uband:
        copy.wait_send()


def on_device(
    start_iterate,
    right_side,
    diag_table,
    inverse_table,
    coupling_tiles,
    diag_index,
    tile_index,
    source_owner,
    source_local,
    aggregate_map,
):
    n_band = lax.axis_size("band")
    n_rows = lax.axis_size("rows")
    block_rows = start_iterate.shape[0]
    n_x, n_z = GRID_XZ[n_rows]
    n_zc, n_xy = n_z * CORES, n_x * n_band
    flat = block_rows * NV
    vmem = pltpu.VMEM
    dma = pltpu.SemaphoreType.DMA
    smem = pl.BlockSpec(memory_space=pltpu.SMEM)
    full = pl.BlockSpec(memory_space=pltpu.VMEM)
    scratch = [
        vmem((block_rows, NV, PH), F32),
        vmem(diag_table.shape, F32),
        vmem(diag_table.shape, F32),
        vmem(diag_table.shape, F32),
        dma((6,)),
        vmem((NT * PH, 2 * PH), BF16),
        vmem((NT * PH, 2 * PH), BF16),
        vmem((4 * NT, PH), BF16),
        vmem((NT, 1, PH), F32),
        vmem((flat, NT * PH), BF16),
        vmem((flat // 2, PH), F32),
        vmem((n_rows, 1, PH), I32),
        vmem((n_rows, 1, PH), I32),
        vmem((1, 1, PH), I32),
        pltpu.SMEM((n_rows, 1, PH), I32),
        pltpu.SMEM((1, 1, PH), I32),
        vmem((1, 1, PH), F32),
        vmem((n_zc, 1, PH), F32),
        vmem((n_xy, 1, PH), F32),
        vmem((n_xy * block_rows, n_zc * block_rows), BF16),
        vmem((1, 4, PH), F32),
        vmem((1, 4, PH), F32),
        vmem((2, n_zc, 4, PH), F32),
        vmem((2, n_xy, 4, PH), F32),
        vmem((n_zc * block_rows, PH), F32),
        vmem((n_xy * block_rows, PH), F32),
        vmem((2, n_xy, 4, PH), F32),
        vmem((2, PARTS, 2 * n_rows, HALF, PH), F32),
        vmem((2 * n_rows, HALF, PH), F32),
        vmem((2 * n_rows, HALF, PH), F32),
        vmem((2 * n_rows, HALF, PH), F32),
        vmem((2 * n_rows, HALF, PH), F32),
        vmem((2, PARTS, block_rows, HALF, PH), F32),
        vmem((2, PARTS, block_rows, HALF, PH), F32),
        vmem((block_rows, HALF, PH), F32),
        vmem((block_rows, HALF, PH), F32),
        vmem((block_rows, HALF, PH), F32),
        vmem((block_rows, HALF, PH), F32),
        vmem((2, 2 * n_rows * NV, PH), BF16),
        vmem((n_rows // 4, 1, PH), F32),
        vmem((n_rows, 1, PH), F32),
        vmem((NT, flat), F32),
        vmem((NT, flat), F32),
        vmem((NT, flat), F32),
        vmem((block_rows, 1, PH), F32),
        dma((2,)),
        dma((2, 2)),
        dma((2, PARTS, 2)),
        dma((2, PARTS, 2, 2)),
        dma((2,)),
        dma((2, 2)),
        dma((2, 2)),
        dma((2, 2)),
        dma((2,)),
    ]
    return pl.pallas_call(
        functools.partial(kernel, n_band, n_rows),
        out_shape=jax.ShapeDtypeStruct(start_iterate.shape, F32),
        in_specs=[smem] * 5 + [pl.BlockSpec(memory_space=pl.ANY)] * 5,
        out_specs=full,
        scratch_shapes=scratch,
        compiler_params=pltpu.CompilerParams(
            collective_id=0, has_side_effects=True, vmem_limit_bytes=67043328
        ),
    )(
        diag_index,
        tile_index.T,
        source_owner.T,
        source_local.T,
        aggregate_map.T,
        start_iterate,
        right_side,
        diag_table,
        inverse_table,
        coupling_tiles,
    )


def solution(mesh):
    in_specs = (
        P(("band", "rows"), None, None),
        P(("band", "rows"), None, None),
        P(),
        P(),
        P(),
        P(("band", "rows")),
        P(("band", "rows"), None),
        P(("band", "rows"), None),
        P(("band", "rows"), None),
        P(("band", "rows"), None),
    )
    out_specs = P(("band", "rows"), None, None)
    return jax.shard_map(
        on_device, mesh=mesh, in_specs=in_specs, out_specs=out_specs, check_vma=False
    )
```

```python
import functools
import jax
import jax.numpy as jnp
from jax import lax
from jax.experimental import pallas as pl
from jax.experimental.pallas import tpu as pltpu
from jax.sharding import PartitionSpec as P

MESH = pl.DeviceIdType.MESH
F32 = jnp.float32
BF16 = jnp.bfloat16
I32 = jnp.int32
PH = 128
NV = 16
HALF = 8
PARTS = NV // HALF
NT = 8
CORES = 2
GRID_XZ = {64: (4, 8), 8: (2, 2)}


def iota(shape, dim):
    return lax.broadcasted_iota(I32, shape, dim)


def best(trips):
    return max(n for n in range(1, 10) if trips % n == 0)


def split(value):
    high = value.astype(BF16)
    return high, (value - high.astype(F32)).astype(BF16)


def nt_dot(a, b):
    return lax.dot_general(a, b, (((1,), (1,)), ((), ())), preferred_element_type=F32)


def dot(a, b):
    return jnp.dot(a, b, preferred_element_type=F32)


def kernel(
    n_band,
    n_rows,
    diag_s,
    tile_s,
    owner_s,
    local_s,
    agg_s,
    v_hbm,
    rhs_hbm,
    dtab_hbm,
    itab_hbm,
    ttab_hbm,
    out_ref,
    rhs_ref,
    dtab,
    itab,
    ttab,
    in_sem,
    tile_mask,
    diag_mask,
    tst,
    ist,
    cols,
    colt,
    whl,
    xs,
    msg,
    slots_v,
    reqs_s,
    slots_s,
    agg_row,
    meta_s,
    meta_t,
    match,
    bs_flat,
    res_flat,
    stage_a,
    stage_b,
    stage_m,
    stage_p,
    stage_o,
    send_big,
    arrived_00,
    arrived_01,
    arrived_10,
    arrived_11,
    low,
    up,
    field_00,
    field_01,
    field_10,
    field_11,
    xhl,
    send_small,
    recv_small,
    u_send,
    u_low,
    u_up,
    zbuf,
    req_sem,
    agg_sem,
    big_sem,
    band_sem,
    small_sem,
    uband_sem,
    a_sem,
    b_sem,
    loc_sem,
):
    arrived = ((arrived_00, arrived_01), (arrived_10, arrived_11))
    field = ((field_00, field_01), (field_10, field_11))
    n_x, n_z = GRID_XZ[n_rows]
    n_zc = n_z * CORES
    n_xy = n_x * n_band
    block_rows = v_hbm.shape[0]
    flat = block_rows * NV
    b = lax.axis_index("band")
    r = lax.axis_index("rows")
    x = r // n_zc
    z = (r // CORES) % n_z
    c = r % CORES
    n_xc = n_x * CORES
    zc = r % n_zc
    xy = x * n_band + b
    below = (b + n_band - 1) % n_band
    above = (b + 1) % n_band

    def turn_peers(turn, sign):
        odd = lax.rem(turn, 2)
        dz = odd * lax.div(turn + 1, 2) + (1 - odd) * (n_z - lax.div(turn, 2))
        pz = lax.rem(z + sign * dz + 2 * n_z, n_z)
        peers = []
        for m in range(n_xc):
            px = lax.rem(x + sign * (m // CORES) + n_x, n_x)
            peers.append((px * n_z + pz) * CORES + lax.rem(c + m % CORES, CORES))
        return peers

    def step_of(owner):
        dx = lax.rem(x - lax.div(owner, n_zc) + n_x, n_x)
        dz = lax.rem(z - lax.rem(lax.div(owner, CORES), n_z) + n_z, n_z)
        dc = lax.rem(c + owner, CORES)
        turn = jnp.where(dz == 0, 0, jnp.where(2 * dz <= n_z, 2 * dz - 1, 2 * (n_z - dz)))
        return turn * n_xc + dx * CORES + dc

    def zc_peer(step):
        return (b, x * n_zc + lax.rem(zc + step, n_zc))

    def xy_peer(step):
        peer = lax.rem(xy + step, n_xy)
        return (lax.rem(peer, n_band), lax.div(peer, n_band) * n_zc + zc)

    loads = [
        pltpu.make_async_copy(source, target, in_sem.at[n])
        for n, (source, target) in enumerate(
            (
                (v_hbm.at[:, 0:HALF, :], field_00),
                (v_hbm.at[:, HALF:NV, :], field_01),
                (ttab_hbm, ttab),
                (dtab_hbm, dtab),
                (itab_hbm, itab),
                (rhs_hbm, rhs_ref),
            )
        )
    ]
    for load in loads:
        load.start()

    barrier = pltpu.get_barrier_semaphore()

    def greet_planes(step, carry):
        py = lax.rem(b + 1 + lax.div(step, n_x), n_band)
        px = lax.rem(x + step, n_x)
        pl.semaphore_signal(barrier, inc=1, device_id=(py, px * n_zc + zc), device_id_type=MESH)
        return carry

    lax.fori_loop(0, n_x * (n_band - 1), greet_planes, 0, unroll=best(n_x * (n_band - 1)))

    def greet_rows(step, carry):
        pl.semaphore_signal(barrier, inc=1, device_id=(b, lax.rem(r + step, n_rows)), device_id_type=MESH)
        return carry

    lax.fori_loop(1, n_rows, greet_rows, 0, unroll=best(n_rows - 1))

    sub = iota((n_rows, PH), 0)
    lane = iota((n_rows, PH), 1)
    lane1 = iota((1, PH), 1)
    parity = lane % 2
    is_local = (lane1 % 4) < 2
    lane_flat = iota((1, flat), 1) // NV

    def collect(i, carry):
        wants, count, slots, aggs, dflat, lowflat, upflat = carry
        for k in range(2):
            off = step_of(owner_s[k, i])
            hit = sub == off
            value = jnp.where(is_local, local_s[k, i], tile_s[k, i])
            wants = jnp.where(hit & (count == parity), value, wants)
            rank = jnp.sum(jnp.where(hit & (count > 0), 1, 0), axis=0, keepdims=True)
            slots = jnp.where(lane1 == 2 * i + k, off * 2 + jnp.clip(rank, 0, 1), slots)
            count = count + hit.astype(I32)
        here = lane_flat == i
        aggs = jnp.where(lane1 % block_rows == i, agg_s[0, i], aggs)
        dflat = jnp.where(here, diag_s[i], dflat)
        lowflat = jnp.where(here, tile_s[2, i], lowflat)
        upflat = jnp.where(here, tile_s[3, i], upflat)
        return wants, count, slots, aggs, dflat, lowflat, upflat

    zero_rows = jnp.zeros((n_rows, PH), I32)
    zero_row = jnp.zeros((1, PH), I32)
    zero_flat = jnp.zeros((1, flat), I32)
    wants, _, slots, aggs, dflat, lowflat, upflat = lax.fori_loop(
        0, block_rows, collect, (zero_rows, zero_rows, zero_row, zero_row, zero_flat, zero_flat, zero_flat)
    )
    for off in range(n_rows):
        msg[off] = wants[off : off + 1, :]
    slots_v[0] = slots
    agg_row[0] = aggs.astype(F32)
    meta_s[pl.ds(zc, 1)] = aggs.astype(F32)[None]
    meta_t[pl.ds(xy, 1)] = aggs.astype(F32)[None]
    slot_copy = pltpu.make_async_copy(slots_v, slots_s, loc_sem.at[0])
    slot_copy.start()
    req_copy = pltpu.make_async_copy(msg.at[pl.ds(0, 1)], reqs_s.at[pl.ds(0, 1)], loc_sem.at[1])
    req_copy.start()

    for load in loads[:4]:
        load.wait()
    col_t = jnp.concatenate([jnp.sum(ttab[t], axis=0, keepdims=True) for t in range(NT)], axis=0)
    col_d = jnp.concatenate([jnp.sum(dtab[t], axis=0, keepdims=True) for t in range(NT)], axis=0)
    for t in range(NT):
        colt[t] = col_t[t : t + 1, :]
    cols[...] = jnp.concatenate(split(col_t) + split(col_d), axis=0)
    table_sum = jnp.sum(col_d, axis=1, keepdims=True)
    sub8 = iota((NT, flat), 0)
    block_sum = jnp.sum(jnp.where(sub8 == dflat, table_sum, 0.0), axis=0, keepdims=True)
    for q in range(4):
        bs_flat[0, q : q + 1, :] = block_sum[:, q * PH : (q + 1) * PH]
    stage_a[0, pl.ds(zc, 1)] = bs_flat[...]

    pl.semaphore_wait(barrier, n_rows - 1 + n_x * (n_band - 1))

    def rows_copies(source, target, width, send_sem, recv_sem, sign, first=0, last=n_z - 1):
        def start(turn, skip):
            for m, peer in enumerate(turn_peers(turn, sign)):
                if m < skip:
                    continue
                step = turn * n_xc + m
                pltpu.make_async_remote_copy(
                    src_ref=source(step),
                    dst_ref=target.at[pl.ds(step * width, width)],
                    send_sem=send_sem,
                    recv_sem=recv_sem,
                    device_id=(b, peer),
                    device_id_type=MESH,
                ).start()

        def one(n, carry):
            start(last - n, 0)
            return carry

        lowest = max(first, 1)
        lax.fori_loop(0, last - lowest + 1, one, 0)
        if first == 0:
            start(0, 1)

    def drain(ref, count, sems):
        part = ref.at[pl.ds(0, count)]
        pltpu.make_async_copy(part, part, sems.at[0]).wait()

    def arrive(ref, count, sems):
        part = ref.at[pl.ds(0, count)]
        pltpu.make_async_copy(part, part, sems.at[1]).wait()

    def band_copies(source, to_above, to_below, sems):
        copies = []
        for side, (target, peer) in enumerate(((to_above, above), (to_below, below))):
            copy = pltpu.make_async_remote_copy(
                src_ref=source,
                dst_ref=target,
                send_sem=sems.at[side, 0],
                recv_sem=sems.at[side, 1],
                device_id=(peer, r),
                device_id_type=MESH,
            )
            copy.start()
            copies.append(copy)
        return copies

    near = min(3, n_z)
    request = lambda step: msg.at[pl.ds(step, 1)]
    rows_copies(request, reqs_s, 1, req_sem.at[0], req_sem.at[2], -1, near, n_z - 1)
    rows_copies(request, reqs_s, 1, req_sem.at[0], req_sem.at[1], -1, 0, near - 1)

    def group_copies(source, target, index, peer_of, count, sems):
        def start(step, carry):
            pltpu.make_async_remote_copy(
                src_ref=source(step),
                dst_ref=target.at[pl.ds(index, 1)],
                send_sem=sems.at[0],
                recv_sem=sems.at[1],
                device_id=peer_of(step),
                device_id_type=MESH,
            ).start()
            return carry

        lax.fori_loop(1, count, start, 0, unroll=True)

    group_copies(lambda step: agg_row, meta_s, zc, zc_peer, n_zc, agg_sem.at[0])
    group_copies(lambda step: agg_row, meta_t, xy, xy_peer, n_xy, agg_sem.at[1])
    group_copies(lambda step: bs_flat, stage_a.at[0], zc, zc_peer, n_zc, a_sem.at[0])

    def share_band(which, part):
        return band_copies(
            field[which][part],
            low.at[which].at[part],
            up.at[which].at[part],
            band_sem.at[which].at[part],
        )

    bands = [[share_band(0, part) for part in range(PARTS)], []]

    def prepare(t, carry):
        rows = pl.ds(pl.multiple_of(t * PH, PH), PH)
        for source, target in ((ttab, tst), (itab, ist)):
            high, rest = split(jnp.transpose(source[t]))
            target[rows, 0:PH] = high
            target[rows, PH : 2 * PH] = rest
        return carry

    def send_blocks(which, part, first=0, last=n_z - 1):
        source = field[which][part]
        buffer = send_big.at[which].at[part]

        def gather(off, carry):
            for rank in range(2):
                buffer[2 * off + rank] = source[reqs_s[off, 0, rank]]
            return carry

        lax.fori_loop(first * n_xc, (last + 1) * n_xc, gather, 0, unroll=4)
        if first == 0:
            arrived[which][part][0:2] = buffer[0:2]
        sems = big_sem.at[which].at[part]
        rows_copies(
            lambda step: buffer.at[pl.ds(2 * step, 2)],
            arrived[which][part],
            2,
            sems.at[0],
            sems.at[1],
            1,
            first,
            last,
        )

    req_copy.wait()
    part_near = reqs_s.at[pl.ds(0, near * n_xc - 1)]
    pltpu.make_async_copy(part_near, part_near, req_sem.at[1]).wait()
    send_blocks(0, 0, 0, near - 1)
    part_far = reqs_s.at[pl.ds(0, (n_z - near) * n_xc)]
    pltpu.make_async_copy(part_far, part_far, req_sem.at[2]).wait()
    send_blocks(0, 0, near, n_z - 1)
    send_blocks(0, 1)
    slot_copy.wait()
    for load in loads[4:]:
        load.wait()
    lax.fori_loop(0, NT, prepare, 0)
    size = block_rows * HALF
    sub_tile = iota((NT, PH), 0)

    def make_masks(i, carry):
        tiles = (
            tile_s[0, i],
            tile_s[1, i],
            jnp.where(b == 0, -1, tile_s[2, i]),
            jnp.where(b == n_band - 1, -1, tile_s[3, i]),
        )
        for k in range(4):
            tile_mask[4 * i + k] = jnp.where(sub_tile == tiles[k], 1.0, 0.0)
        diag_mask[i] = jnp.where(sub_tile == diag_s[i], 1.0, 0.0)
        return carry

    lax.fori_loop(0, block_rows, make_masks, 0, unroll=4)

    def coupled_apply(which, part, target):
        arrive(arrived[which][part], 2 * (n_rows - 1), big_sem.at[which].at[part])
        for copy in bands[which][part]:
            copy.wait_recv()
        columns = slice(part * HALF, (part + 1) * HALF)

        def form(pair, carry):
            rows = pl.ds(pl.multiple_of(pair * NV, NV), NV)
            rest_rows = pl.ds(pl.multiple_of(size + pair * NV, NV), NV)
            sums = []
            for i in (2 * pair, 2 * pair + 1):
                sources = (
                    arrived[which][part][slots_s[0, 0, 2 * i]],
                    arrived[which][part][slots_s[0, 0, 2 * i + 1]],
                    low[which, part, i],
                    up[which, part, i],
                )
                totals = []
                for t in range(NT):
                    total = tile_mask[4 * i, t : t + 1, :] * sources[0]
                    for k in range(1, 4):
                        total = total + tile_mask[4 * i + k, t : t + 1, :] * sources[k]
                    totals.append(total)
                sums.append(totals)
            for t in range(NT):
                high, rest = split(jnp.concatenate([sums[0][t], sums[1][t]], axis=0))
                whl[rows, t * PH : (t + 1) * PH] = high
                whl[rest_rows, t * PH : (t + 1) * PH] = rest
            return carry

        lax.fori_loop(0, block_rows // 2, form, 0)
        y = dot(whl[...], tst[...])
        y = y[:size] + y[size:]
        xs[...] = rhs_ref[:, columns, :].reshape(size, PH) + (y[:, :PH] + y[:, PH:])

        def form_diag(pair, carry):
            rows = pl.ds(pl.multiple_of(pair * NV, NV), NV)
            rest_rows = pl.ds(pl.multiple_of(size + pair * NV, NV), NV)
            value = xs[rows, :]
            rest = value - value.astype(BF16).astype(F32)
            for t in range(NT):
                keep = [diag_mask[2 * pair + n, t : t + 1, :] for n in range(2)]
                for source, place in ((value, rows), (rest, rest_rows)):
                    kept = jnp.concatenate(
                        [source[:HALF] * keep[0], source[HALF:] * keep[1]], axis=0
                    )
                    whl[place, t * PH : (t + 1) * PH] = kept.astype(BF16)
            return carry

        lax.fori_loop(0, block_rows // 2, form_diag, 0)
        y = dot(whl[...], ist[...])
        y = y[:size] + y[size:]
        target[...] = (y[:, :PH] + y[:, PH:]).reshape(block_rows, HALF, PH)

    arrive(meta_s, n_zc - 1, agg_sem.at[0])
    arrive(meta_t, n_xy - 1, agg_sem.at[1])
    lanes = iota((1, PH), 1)
    per_row = PH // block_rows
    pieces = []
    for group in range(n_zc // per_row):
        piece = jnp.zeros((1, PH), F32)
        for place in range(per_row):
            piece = jnp.where(lanes // block_rows == place, meta_s[group * per_row + place], piece)
        pieces.append(piece)
    source_row = jnp.concatenate(pieces, axis=1)
    own_lane = iota((block_rows, PH), 1) == iota((block_rows, PH), 0)

    def build(d, carry):
        column = jnp.sum(jnp.where(own_lane, meta_t[d], 0.0), axis=1, keepdims=True)
        rows = pl.ds(pl.multiple_of(d * block_rows, block_rows), block_rows)
        match[rows, :] = jnp.where(column == source_row, 1.0, 0.0).astype(BF16)
        return carry

    lax.fori_loop(0, n_xy, build, 0, unroll=2)
    block_lane = (iota((8, PH), 1) // NV) == iota((8, PH), 0)
    fold = jnp.where(iota((PH, PH), 0) % NV == iota((PH, PH), 1) % NV, 1.0, 0.0).astype(BF16)

    def fold_lanes(value):
        high, rest = split(value)
        return dot(high, fold) + dot(rest, fold)

    def to_flat_rows(value, q):
        picked = jnp.where(block_lane, value[q * 8 : (q + 1) * 8, :], 0.0)
        return jnp.sum(picked, axis=0, keepdims=True)

    def partial_sums(which):
        arrive(stage_a.at[which], n_zc - 1, a_sem.at[which])

        def spread(source, carry):
            value = stage_a[which, source]
            for q in range(4):
                rows = pl.ds(pl.multiple_of(source * block_rows + q * 8, 8), 8)
                stage_m[rows, :] = jnp.where(block_lane, value[q : q + 1, :], 0.0)
            return carry

        lax.fori_loop(0, n_zc, spread, 0, unroll=4)
        both = jnp.concatenate(split(stage_m[...]), axis=1)
        y = dot(match[...], both)
        stage_p[...] = fold_lanes(y[:, :PH] + y[:, PH:])

        def flatten(d, carry):
            value = stage_p[pl.ds(pl.multiple_of(d * block_rows, block_rows), block_rows), :]
            for q in range(4):
                stage_o[which, d, q : q + 1, :] = to_flat_rows(value, q)
            return carry

        lax.fori_loop(0, n_xy, flatten, 0, unroll=4)
        stage_b[which, pl.ds(xy, 1)] = stage_o[which, pl.ds(xy, 1)]

        def out_part(step):
            return stage_o.at[which].at[pl.ds(lax.rem(xy + step, n_xy), 1)]

        group_copies(out_part, stage_b.at[which], xy, xy_peer, n_xy, b_sem.at[which])

    partial_sums(0)

    for part in range(PARTS):
        coupled_apply(0, part, field[1][part])
        send_blocks(1, part)
        bands[1].append(share_band(1, part))
    ones = jnp.ones((8, PH), BF16)
    rhs_parts = split(rhs_ref[...].reshape(flat, PH))
    rhs_sum = (nt_dot(ones, rhs_parts[0]) + nt_dot(ones, rhs_parts[1]))[0:1, :]
    for part in range(PARTS):
        coupled_apply(1, part, out_ref.at[:, part * HALF : (part + 1) * HALF, :])

    second_parts = split(out_ref[...].reshape(flat, PH))
    projected = nt_dot(cols[...], second_parts[0]) + nt_dot(cols[...], second_parts[1])
    u_send[...] = projected[0:8] + projected[8:16]
    uband = band_copies(u_send, u_low, u_up, uband_sem)

    def edge(off, carry):
        for rank in range(2):
            value = out_ref[reqs_s[off, 0, rank]] * colt[reqs_s[off, 0, 2 + rank]]
            high, rest = split(value)
            place = pl.ds(pl.multiple_of((2 * off + rank) * NV, NV), NV)
            xhl[0, place, :] = high
            xhl[1, place, :] = rest
        return carry

    lax.fori_loop(0, n_rows, edge, 0, unroll=4)
    edges = nt_dot(ones, xhl[0]) + nt_dot(ones, xhl[1])
    for group in range(n_rows // 4):
        send_small[group] = edges[0:1, group * PH : (group + 1) * PH]
    recv_small[0] = edges[0:1, 0:PH]
    rows_copies(lambda step: send_small.at[pl.ds(lax.div(step, 4), 1)], recv_small, 1, small_sem.at[0], small_sem.at[1], 1)

    own = projected[16:24] + projected[24:32]
    local_sum = rhs_sum - jnp.sum(jnp.where(sub8 == dflat, own, 0.0), axis=0, keepdims=True)
    for copy in uband:
        copy.wait_recv()
    has_low = jnp.where(b == 0, 0.0, 1.0)
    has_up = jnp.where(b == n_band - 1, 0.0, 1.0)
    local_sum = local_sum + has_low * jnp.sum(
        jnp.where(sub8 == lowflat, u_low[...], 0.0), axis=0, keepdims=True
    )
    local_sum = local_sum + has_up * jnp.sum(
        jnp.where(sub8 == upflat, u_up[...], 0.0), axis=0, keepdims=True
    )
    arrive(recv_small, n_rows - 1, small_sem)

    def collect_edges(i, carry):
        total = jnp.zeros((1, PH), F32)
        for k in range(2):
            slot = slots_s[0, 0, 2 * i + k]
            piece = recv_small[slot // 2]
            total = total + jnp.where(lanes // NV == slot % 8, piece, 0.0)
        zbuf[i] = total
        return carry

    lax.fori_loop(0, block_rows, collect_edges, 0, unroll=4)
    rows_of = fold_lanes(zbuf[...].reshape(block_rows, PH))
    for q in range(4):
        res_flat[0, q : q + 1, :] = local_sum[:, q * PH : (q + 1) * PH] + to_flat_rows(rows_of, q)
    stage_a[1, pl.ds(zc, 1)] = res_flat[...]
    group_copies(lambda step: res_flat, stage_a.at[1], zc, zc_peer, n_zc, a_sem.at[1])
    partial_sums(1)

    arrive(stage_b.at[0], n_xy - 1, b_sem.at[0])
    denominator = jnp.sum(stage_b[0], axis=0)
    arrive(stage_b.at[1], n_xy - 1, b_sem.at[1])
    correction = jnp.sum(stage_b[1], axis=0) / denominator
    eye = iota((PH, PH), 0) == iota((PH, PH), 1)
    for q in range(4):
        column = jnp.sum(jnp.where(eye, correction[q : q + 1, :], 0.0), axis=1, keepdims=True)
        out_ref[q * 8 : (q + 1) * 8] = out_ref[q * 8 : (q + 1) * 8] + column.reshape(8, NV, 1)

    drain(msg, n_rows - 1, req_sem)
    drain(meta_s, n_zc - 1, agg_sem.at[0])
    drain(meta_t, n_xy - 1, agg_sem.at[1])
    for which in range(2):
        for part in range(PARTS):
            drain(send_big.at[which].at[part], 2 * (n_rows - 1), big_sem.at[which].at[part])
            for copy in bands[which][part]:
                copy.wait_send()
        drain(stage_a.at[which], n_zc - 1, a_sem.at[which])
        drain(stage_o.at[which], n_xy - 1, b_sem.at[which])
    drain(recv_small, n_rows - 1, small_sem)
    for copy in uband:
        copy.wait_send()


def on_device(
    start_iterate,
    right_side,
    diag_table,
    inverse_table,
    coupling_tiles,
    diag_index,
    tile_index,
    source_owner,
    source_local,
    aggregate_map,
):
    n_band = lax.axis_size("band")
    n_rows = lax.axis_size("rows")
    block_rows = start_iterate.shape[0]
    n_x, n_z = GRID_XZ[n_rows]
    n_zc, n_xy = n_z * CORES, n_x * n_band
    flat = block_rows * NV
    vmem = pltpu.VMEM
    dma = pltpu.SemaphoreType.DMA
    smem = pl.BlockSpec(memory_space=pltpu.SMEM)
    full = pl.BlockSpec(memory_space=pltpu.VMEM)
    scratch = [
        vmem((block_rows, NV, PH), F32),
        vmem(diag_table.shape, F32),
        vmem(diag_table.shape, F32),
        vmem(diag_table.shape, F32),
        dma((6,)),
        vmem((4 * block_rows, NT, PH), F32),
        vmem((block_rows, NT, PH), F32),
        vmem((NT * PH, 2 * PH), BF16),
        vmem((NT * PH, 2 * PH), BF16),
        vmem((4 * NT, PH), BF16),
        vmem((NT, 1, PH), F32),
        vmem((flat, NT * PH), BF16),
        vmem((flat // 2, PH), F32),
        vmem((n_rows, 1, PH), I32),
        vmem((1, 1, PH), I32),
        pltpu.SMEM((n_rows, 1, PH), I32),
        pltpu.SMEM((1, 1, PH), I32),
        vmem((1, 1, PH), F32),
        vmem((n_zc, 1, PH), F32),
        vmem((n_xy, 1, PH), F32),
        vmem((n_xy * block_rows, n_zc * block_rows), BF16),
        vmem((1, 4, PH), F32),
        vmem((1, 4, PH), F32),
        vmem((2, n_zc, 4, PH), F32),
        vmem((2, n_xy, 4, PH), F32),
        vmem((n_zc * block_rows, PH), F32),
        vmem((n_xy * block_rows, PH), F32),
        vmem((2, n_xy, 4, PH), F32),
        vmem((2, PARTS, 2 * n_rows, HALF, PH), F32),
        vmem((2 * n_rows, HALF, PH), F32),
        vmem((2 * n_rows, HALF, PH), F32),
        vmem((2 * n_rows, HALF, PH), F32),
        vmem((2 * n_rows, HALF, PH), F32),
        vmem((2, PARTS, block_rows, HALF, PH), F32),
        vmem((2, PARTS, block_rows, HALF, PH), F32),
        vmem((block_rows, HALF, PH), F32),
        vmem((block_rows, HALF, PH), F32),
        vmem((block_rows, HALF, PH), F32),
        vmem((block_rows, HALF, PH), F32),
        vmem((2, 2 * n_rows * NV, PH), BF16),
        vmem((n_rows // 4, 1, PH), F32),
        vmem((n_rows, 1, PH), F32),
        vmem((NT, flat), F32),
        vmem((NT, flat), F32),
        vmem((NT, flat), F32),
        vmem((block_rows, 1, PH), F32),
        dma((3,)),
        dma((2, 2)),
        dma((2, PARTS, 2)),
        dma((2, PARTS, 2, 2)),
        dma((2,)),
        dma((2, 2)),
        dma((2, 2)),
        dma((2, 2)),
        dma((2,)),
    ]
    return pl.pallas_call(
        functools.partial(kernel, n_band, n_rows),
        out_shape=jax.ShapeDtypeStruct(start_iterate.shape, F32),
        in_specs=[smem] * 5 + [pl.BlockSpec(memory_space=pl.ANY)] * 5,
        out_specs=full,
        scratch_shapes=scratch,
        compiler_params=pltpu.CompilerParams(
            collective_id=0, has_side_effects=True, vmem_limit_bytes=67043328
        ),
    )(
        diag_index,
        tile_index.T,
        source_owner.T,
        source_local.T,
        aggregate_map.T,
        start_iterate,
        right_side,
        diag_table,
        inverse_table,
        coupling_tiles,
    )


def solution(mesh):
    in_specs = (
        P(("band", "rows"), None, None),
        P(("band", "rows"), None, None),
        P(),
        P(),
        P(),
        P(("band", "rows")),
        P(("band", "rows"), None),
        P(("band", "rows"), None),
        P(("band", "rows"), None),
        P(("band", "rows"), None),
    )
    out_specs = P(("band", "rows"), None, None)
    return jax.shard_map(
        on_device, mesh=mesh, in_specs=in_specs, out_specs=out_specs, check_vma=False
    )
```

```python
import functools
import jax
import jax.numpy as jnp
from jax import lax
from jax.experimental import pallas as pl
from jax.experimental.pallas import tpu as pltpu
from jax.sharding import PartitionSpec as P

MESH = pl.DeviceIdType.MESH
F32 = jnp.float32
BF16 = jnp.bfloat16
I32 = jnp.int32
PH = 128
NV = 16
HALF = 8
PARTS = NV // HALF
NT = 8
CORES = 2
GRID_XZ = {64: (4, 8), 8: (2, 2)}


def iota(shape, dim):
    return lax.broadcasted_iota(I32, shape, dim)


def best(trips):
    return max(n for n in range(1, 10) if trips % n == 0)


def split(value):
    high = value.astype(BF16)
    return high, (value - high.astype(F32)).astype(BF16)


def nt_dot(a, b):
    return lax.dot_general(a, b, (((1,), (1,)), ((), ())), preferred_element_type=F32)


def dot(a, b):
    return jnp.dot(a, b, preferred_element_type=F32)


def kernel(
    n_band,
    n_rows,
    diag_hbm,
    tile_hbm,
    owner_hbm,
    local_hbm,
    agg_hbm,
    v_hbm,
    rhs_hbm,
    dtab_hbm,
    itab_hbm,
    ttab_hbm,
    out_ref,
    rhs_ref,
    dtab,
    itab,
    ttab,
    in_sem,
    diag_s,
    tile_s,
    owner_s,
    local_s,
    agg_s,
    index_sem,
    tile_mask,
    diag_mask,
    tst,
    ist,
    cols,
    colt,
    whl,
    xs,
    msg,
    slots_v,
    reqs_s,
    slots_s,
    agg_row,
    meta_s,
    meta_t,
    match,
    bs_flat,
    res_flat,
    stage_a,
    stage_b,
    stage_m,
    stage_p,
    stage_o,
    send_big,
    arrived_00,
    arrived_01,
    arrived_10,
    arrived_11,
    low,
    up,
    field_00,
    field_01,
    field_10,
    field_11,
    xhl,
    send_small,
    recv_small,
    u_send,
    u_low,
    u_up,
    zbuf,
    req_sem,
    agg_sem,
    big_sem,
    band_sem,
    small_sem,
    uband_sem,
    a_sem,
    b_sem,
    loc_sem,
):
    arrived = ((arrived_00, arrived_01), (arrived_10, arrived_11))
    field = ((field_00, field_01), (field_10, field_11))
    n_x, n_z = GRID_XZ[n_rows]
    n_zc = n_z * CORES
    n_xy = n_x * n_band
    block_rows = v_hbm.shape[0]
    flat = block_rows * NV
    b = lax.axis_index("band")
    r = lax.axis_index("rows")
    x = r // n_zc
    z = (r // CORES) % n_z
    c = r % CORES
    n_xc = n_x * CORES
    zc = r % n_zc
    xy = x * n_band + b
    below = (b + n_band - 1) % n_band
    above = (b + 1) % n_band

    def turn_peers(turn, sign):
        odd = lax.rem(turn, 2)
        dz = odd * lax.div(turn + 1, 2) + (1 - odd) * (n_z - lax.div(turn, 2))
        pz = lax.rem(z + sign * dz + 2 * n_z, n_z)
        peers = []
        for m in range(n_xc):
            px = lax.rem(x + sign * (m // CORES) + n_x, n_x)
            peers.append((px * n_z + pz) * CORES + lax.rem(c + m % CORES, CORES))
        return peers

    def step_of(owner):
        dx = lax.rem(x - lax.div(owner, n_zc) + n_x, n_x)
        dz = lax.rem(z - lax.rem(lax.div(owner, CORES), n_z) + n_z, n_z)
        dc = lax.rem(c + owner, CORES)
        turn = jnp.where(dz == 0, 0, jnp.where(2 * dz <= n_z, 2 * dz - 1, 2 * (n_z - dz)))
        return turn * n_xc + dx * CORES + dc

    def zc_peer(step):
        return (b, x * n_zc + lax.rem(zc + step, n_zc))

    def xy_peer(step):
        peer = lax.rem(xy + step, n_xy)
        return (lax.rem(peer, n_band), lax.div(peer, n_band) * n_zc + zc)

    loads = [
        pltpu.make_async_copy(source, target, in_sem.at[n])
        for n, (source, target) in enumerate(
            (
                (v_hbm.at[:, 0:HALF, :], field_00),
                (v_hbm.at[:, HALF:NV, :], field_01),
                (ttab_hbm, ttab),
                (dtab_hbm, dtab),
                (itab_hbm, itab),
                (rhs_hbm, rhs_ref),
            )
        )
    ]
    index_loads = [
        pltpu.make_async_copy(source, target, index_sem.at[n])
        for n, (source, target) in enumerate(
            (
                (diag_hbm, diag_s),
                (tile_hbm, tile_s),
                (owner_hbm, owner_s),
                (local_hbm, local_s),
                (agg_hbm, agg_s),
            )
        )
    ]
    for load in index_loads + loads:
        load.start()

    barrier = pltpu.get_barrier_semaphore()

    def greet_planes(step, carry):
        py = lax.rem(b + 1 + lax.div(step, n_x), n_band)
        px = lax.rem(x + step, n_x)
        pl.semaphore_signal(barrier, inc=1, device_id=(py, px * n_zc + zc), device_id_type=MESH)
        return carry

    lax.fori_loop(0, n_x * (n_band - 1), greet_planes, 0, unroll=best(n_x * (n_band - 1)))

    def greet_rows(step, carry):
        pl.semaphore_signal(barrier, inc=1, device_id=(b, lax.rem(r + step, n_rows)), device_id_type=MESH)
        return carry

    lax.fori_loop(1, n_rows, greet_rows, 0, unroll=best(n_rows - 1))

    for load in index_loads:
        load.wait()
    sub = iota((n_rows, PH), 0)
    lane = iota((n_rows, PH), 1)
    lane1 = iota((1, PH), 1)
    parity = lane % 2
    is_local = (lane1 % 4) < 2
    lane_flat = iota((1, flat), 1) // NV

    def collect(i, carry):
        wants, count, slots, aggs, dflat, lowflat, upflat = carry
        for k in range(2):
            off = step_of(owner_s[k, i])
            hit = sub == off
            value = jnp.where(is_local, local_s[k, i], tile_s[k, i])
            wants = jnp.where(hit & (count == parity), value, wants)
            rank = jnp.sum(jnp.where(hit & (count > 0), 1, 0), axis=0, keepdims=True)
            slots = jnp.where(lane1 == 2 * i + k, off * 2 + jnp.clip(rank, 0, 1), slots)
            count = count + hit.astype(I32)
        here = lane_flat == i
        aggs = jnp.where(lane1 % block_rows == i, agg_s[0, i], aggs)
        dflat = jnp.where(here, diag_s[i], dflat)
        lowflat = jnp.where(here, tile_s[2, i], lowflat)
        upflat = jnp.where(here, tile_s[3, i], upflat)
        return wants, count, slots, aggs, dflat, lowflat, upflat

    zero_rows = jnp.zeros((n_rows, PH), I32)
    zero_row = jnp.zeros((1, PH), I32)
    zero_flat = jnp.zeros((1, flat), I32)
    wants, _, slots, aggs, dflat, lowflat, upflat = lax.fori_loop(
        0, block_rows, collect, (zero_rows, zero_rows, zero_row, zero_row, zero_flat, zero_flat, zero_flat)
    )
    for off in range(n_rows):
        msg[off] = wants[off : off + 1, :]
    slots_v[0] = slots
    agg_row[0] = aggs.astype(F32)
    meta_s[pl.ds(zc, 1)] = aggs.astype(F32)[None]
    meta_t[pl.ds(xy, 1)] = aggs.astype(F32)[None]
    slot_copy = pltpu.make_async_copy(slots_v, slots_s, loc_sem.at[0])
    slot_copy.start()
    req_copy = pltpu.make_async_copy(msg.at[pl.ds(0, 1)], reqs_s.at[pl.ds(0, 1)], loc_sem.at[1])
    req_copy.start()

    for load in loads[:4]:
        load.wait()
    col_t = jnp.concatenate([jnp.sum(ttab[t], axis=0, keepdims=True) for t in range(NT)], axis=0)
    col_d = jnp.concatenate([jnp.sum(dtab[t], axis=0, keepdims=True) for t in range(NT)], axis=0)
    for t in range(NT):
        colt[t] = col_t[t : t + 1, :]
    cols[...] = jnp.concatenate(split(col_t) + split(col_d), axis=0)
    table_sum = jnp.sum(col_d, axis=1, keepdims=True)
    sub8 = iota((NT, flat), 0)
    block_sum = jnp.sum(jnp.where(sub8 == dflat, table_sum, 0.0), axis=0, keepdims=True)
    for q in range(4):
        bs_flat[0, q : q + 1, :] = block_sum[:, q * PH : (q + 1) * PH]
    stage_a[0, pl.ds(zc, 1)] = bs_flat[...]

    pl.semaphore_wait(barrier, n_rows - 1 + n_x * (n_band - 1))

    def rows_copies(source, target, width, send_sem, recv_sem, sign, first=0, last=n_z - 1):
        def start(turn, skip):
            for m, peer in enumerate(turn_peers(turn, sign)):
                if m < skip:
                    continue
                step = turn * n_xc + m
                pltpu.make_async_remote_copy(
                    src_ref=source(step),
                    dst_ref=target.at[pl.ds(step * width, width)],
                    send_sem=send_sem,
                    recv_sem=recv_sem,
                    device_id=(b, peer),
                    device_id_type=MESH,
                ).start()

        def one(n, carry):
            start(last - n, 0)
            return carry

        lowest = max(first, 1)
        lax.fori_loop(0, last - lowest + 1, one, 0)
        if first == 0:
            start(0, 1)

    def drain(ref, count, sems):
        part = ref.at[pl.ds(0, count)]
        pltpu.make_async_copy(part, part, sems.at[0]).wait()

    def arrive(ref, count, sems):
        part = ref.at[pl.ds(0, count)]
        pltpu.make_async_copy(part, part, sems.at[1]).wait()

    def band_copies(source, to_above, to_below, sems):
        copies = []
        for side, (target, peer) in enumerate(((to_above, above), (to_below, below))):
            copy = pltpu.make_async_remote_copy(
                src_ref=source,
                dst_ref=target,
                send_sem=sems.at[side, 0],
                recv_sem=sems.at[side, 1],
                device_id=(peer, r),
                device_id_type=MESH,
            )
            copy.start()
            copies.append(copy)
        return copies

    near = min(3, n_z)
    request = lambda step: msg.at[pl.ds(step, 1)]
    rows_copies(request, reqs_s, 1, req_sem.at[0], req_sem.at[2], -1, near, n_z - 1)
    rows_copies(request, reqs_s, 1, req_sem.at[0], req_sem.at[1], -1, 0, near - 1)

    def group_copies(source, target, index, peer_of, count, sems):
        def start(step, carry):
            pltpu.make_async_remote_copy(
                src_ref=source(step),
                dst_ref=target.at[pl.ds(index, 1)],
                send_sem=sems.at[0],
                recv_sem=sems.at[1],
                device_id=peer_of(step),
                device_id_type=MESH,
            ).start()
            return carry

        lax.fori_loop(1, count, start, 0, unroll=True)

    group_copies(lambda step: agg_row, meta_s, zc, zc_peer, n_zc, agg_sem.at[0])
    group_copies(lambda step: agg_row, meta_t, xy, xy_peer, n_xy, agg_sem.at[1])
    group_copies(lambda step: bs_flat, stage_a.at[0], zc, zc_peer, n_zc, a_sem.at[0])

    def share_band(which, part):
        return band_copies(
            field[which][part],
            low.at[which].at[part],
            up.at[which].at[part],
            band_sem.at[which].at[part],
        )

    bands = [[share_band(0, part) for part in range(PARTS)], []]

    def prepare(t, carry):
        rows = pl.ds(pl.multiple_of(t * PH, PH), PH)
        for source, target in ((ttab, tst), (itab, ist)):
            high, rest = split(jnp.transpose(source[t]))
            target[rows, 0:PH] = high
            target[rows, PH : 2 * PH] = rest
        return carry

    def send_blocks(which, part, first=0, last=n_z - 1):
        source = field[which][part]
        buffer = send_big.at[which].at[part]

        def gather(off, carry):
            for rank in range(2):
                buffer[2 * off + rank] = source[reqs_s[off, 0, rank]]
            return carry

        lax.fori_loop(first * n_xc, (last + 1) * n_xc, gather, 0, unroll=4)
        if first == 0:
            arrived[which][part][0:2] = buffer[0:2]
        sems = big_sem.at[which].at[part]
        rows_copies(
            lambda step: buffer.at[pl.ds(2 * step, 2)],
            arrived[which][part],
            2,
            sems.at[0],
            sems.at[1],
            1,
            first,
            last,
        )

    req_copy.wait()
    part_near = reqs_s.at[pl.ds(0, near * n_xc - 1)]
    pltpu.make_async_copy(part_near, part_near, req_sem.at[1]).wait()
    send_blocks(0, 0, 0, near - 1)
    part_far = reqs_s.at[pl.ds(0, (n_z - near) * n_xc)]
    pltpu.make_async_copy(part_far, part_far, req_sem.at[2]).wait()
    send_blocks(0, 0, near, n_z - 1)
    send_blocks(0, 1)
    slot_copy.wait()
    for load in loads[4:]:
        load.wait()
    lax.fori_loop(0, NT, prepare, 0)
    size = block_rows * HALF
    sub_tile = iota((NT, PH), 0)

    def make_masks(i, carry):
        tiles = (
            tile_s[0, i],
            tile_s[1, i],
            jnp.where(b == 0, -1, tile_s[2, i]),
            jnp.where(b == n_band - 1, -1, tile_s[3, i]),
        )
        for k in range(4):
            tile_mask[4 * i + k] = jnp.where(sub_tile == tiles[k], 1.0, 0.0)
        diag_mask[i] = jnp.where(sub_tile == diag_s[i], 1.0, 0.0)
        return carry

    lax.fori_loop(0, block_rows, make_masks, 0, unroll=4)

    def coupled_apply(which, part, target):
        arrive(arrived[which][part], 2 * (n_rows - 1), big_sem.at[which].at[part])
        for copy in bands[which][part]:
            copy.wait_recv()
        columns = slice(part * HALF, (part + 1) * HALF)

        def form(pair, carry):
            rows = pl.ds(pl.multiple_of(pair * NV, NV), NV)
            rest_rows = pl.ds(pl.multiple_of(size + pair * NV, NV), NV)
            sums = []
            for i in (2 * pair, 2 * pair + 1):
                sources = (
                    arrived[which][part][slots_s[0, 0, 2 * i]],
                    arrived[which][part][slots_s[0, 0, 2 * i + 1]],
                    low[which, part, i],
                    up[which, part, i],
                )
                totals = []
                for t in range(NT):
                    total = tile_mask[4 * i, t : t + 1, :] * sources[0]
                    for k in range(1, 4):
                        total = total + tile_mask[4 * i + k, t : t + 1, :] * sources[k]
                    totals.append(total)
                sums.append(totals)
            for t in range(NT):
                high, rest = split(jnp.concatenate([sums[0][t], sums[1][t]], axis=0))
                whl[rows, t * PH : (t + 1) * PH] = high
                whl[rest_rows, t * PH : (t + 1) * PH] = rest
            return carry

        lax.fori_loop(0, block_rows // 2, form, 0)
        y = dot(whl[...], tst[...])
        y = y[:size] + y[size:]
        xs[...] = rhs_ref[:, columns, :].reshape(size, PH) + (y[:, :PH] + y[:, PH:])

        def form_diag(pair, carry):
            rows = pl.ds(pl.multiple_of(pair * NV, NV), NV)
            rest_rows = pl.ds(pl.multiple_of(size + pair * NV, NV), NV)
            value = xs[rows, :]
            rest = value - value.astype(BF16).astype(F32)
            for t in range(NT):
                keep = [diag_mask[2 * pair + n, t : t + 1, :] for n in range(2)]
                for source, place in ((value, rows), (rest, rest_rows)):
                    kept = jnp.concatenate(
                        [source[:HALF] * keep[0], source[HALF:] * keep[1]], axis=0
                    )
                    whl[place, t * PH : (t + 1) * PH] = kept.astype(BF16)
            return carry

        lax.fori_loop(0, block_rows // 2, form_diag, 0)
        y = dot(whl[...], ist[...])
        y = y[:size] + y[size:]
        target[...] = (y[:, :PH] + y[:, PH:]).reshape(block_rows, HALF, PH)

    arrive(meta_s, n_zc - 1, agg_sem.at[0])
    arrive(meta_t, n_xy - 1, agg_sem.at[1])
    lanes = iota((1, PH), 1)
    per_row = PH // block_rows
    pieces = []
    for group in range(n_zc // per_row):
        piece = jnp.zeros((1, PH), F32)
        for place in range(per_row):
            piece = jnp.where(lanes // block_rows == place, meta_s[group * per_row + place], piece)
        pieces.append(piece)
    source_row = jnp.concatenate(pieces, axis=1)
    own_lane = iota((block_rows, PH), 1) == iota((block_rows, PH), 0)

    def build(d, carry):
        column = jnp.sum(jnp.where(own_lane, meta_t[d], 0.0), axis=1, keepdims=True)
        rows = pl.ds(pl.multiple_of(d * block_rows, block_rows), block_rows)
        match[rows, :] = jnp.where(column == source_row, 1.0, 0.0).astype(BF16)
        return carry

    lax.fori_loop(0, n_xy, build, 0, unroll=2)
    block_lane = (iota((8, PH), 1) // NV) == iota((8, PH), 0)
    fold = jnp.where(iota((PH, PH), 0) % NV == iota((PH, PH), 1) % NV, 1.0, 0.0).astype(BF16)

    def fold_lanes(value):
        high, rest = split(value)
        return dot(high, fold) + dot(rest, fold)

    def to_flat_rows(value, q):
        picked = jnp.where(block_lane, value[q * 8 : (q + 1) * 8, :], 0.0)
        return jnp.sum(picked, axis=0, keepdims=True)

    def partial_sums(which):
        arrive(stage_a.at[which], n_zc - 1, a_sem.at[which])

        def spread(source, carry):
            value = stage_a[which, source]
            for q in range(4):
                rows = pl.ds(pl.multiple_of(source * block_rows + q * 8, 8), 8)
                stage_m[rows, :] = jnp.where(block_lane, value[q : q + 1, :], 0.0)
            return carry

        lax.fori_loop(0, n_zc, spread, 0, unroll=4)
        both = jnp.concatenate(split(stage_m[...]), axis=1)
        y = dot(match[...], both)
        stage_p[...] = fold_lanes(y[:, :PH] + y[:, PH:])

        def flatten(d, carry):
            value = stage_p[pl.ds(pl.multiple_of(d * block_rows, block_rows), block_rows), :]
            for q in range(4):
                stage_o[which, d, q : q + 1, :] = to_flat_rows(value, q)
            return carry

        lax.fori_loop(0, n_xy, flatten, 0, unroll=4)
        stage_b[which, pl.ds(xy, 1)] = stage_o[which, pl.ds(xy, 1)]

        def out_part(step):
            return stage_o.at[which].at[pl.ds(lax.rem(xy + step, n_xy), 1)]

        group_copies(out_part, stage_b.at[which], xy, xy_peer, n_xy, b_sem.at[which])

    partial_sums(0)

    for part in range(PARTS):
        coupled_apply(0, part, field[1][part])
        send_blocks(1, part)
        bands[1].append(share_band(1, part))
    ones = jnp.ones((8, PH), BF16)
    rhs_parts = split(rhs_ref[...].reshape(flat, PH))
    rhs_sum = (nt_dot(ones, rhs_parts[0]) + nt_dot(ones, rhs_parts[1]))[0:1, :]
    for part in range(PARTS):
        coupled_apply(1, part, out_ref.at[:, part * HALF : (part + 1) * HALF, :])

    def edge(off, carry):
        for rank in range(2):
            value = out_ref[reqs_s[off, 0, rank]] * colt[reqs_s[off, 0, 2 + rank]]
            high, rest = split(value)
            place = pl.ds(pl.multiple_of((2 * off + rank) * NV, NV), NV)
            xhl[0, place, :] = high
            xhl[1, place, :] = rest
        return carry

    lax.fori_loop(0, n_rows, edge, 0, unroll=8)
    edges = nt_dot(ones, xhl[0]) + nt_dot(ones, xhl[1])
    for group in range(n_rows // 4):
        send_small[group] = edges[0:1, group * PH : (group + 1) * PH]
    recv_small[0] = edges[0:1, 0:PH]
    rows_copies(lambda step: send_small.at[pl.ds(lax.div(step, 4), 1)], recv_small, 1, small_sem.at[0], small_sem.at[1], 1)

    second_parts = split(out_ref[...].reshape(flat, PH))
    projected = nt_dot(cols[...], second_parts[0]) + nt_dot(cols[...], second_parts[1])
    u_send[...] = projected[0:8] + projected[8:16]
    uband = band_copies(u_send, u_low, u_up, uband_sem)

    own = projected[16:24] + projected[24:32]
    local_sum = rhs_sum - jnp.sum(jnp.where(sub8 == dflat, own, 0.0), axis=0, keepdims=True)
    for copy in uband:
        copy.wait_recv()
    has_low = jnp.where(b == 0, 0.0, 1.0)
    has_up = jnp.where(b == n_band - 1, 0.0, 1.0)
    local_sum = local_sum + has_low * jnp.sum(
        jnp.where(sub8 == lowflat, u_low[...], 0.0), axis=0, keepdims=True
    )
    local_sum = local_sum + has_up * jnp.sum(
        jnp.where(sub8 == upflat, u_up[...], 0.0), axis=0, keepdims=True
    )
    arrive(recv_small, n_rows - 1, small_sem)

    def collect_edges(i, carry):
        total = jnp.zeros((1, PH), F32)
        for k in range(2):
            slot = slots_s[0, 0, 2 * i + k]
            piece = recv_small[slot // 2]
            total = total + jnp.where(lanes // NV == slot % 8, piece, 0.0)
        zbuf[i] = total
        return carry

    lax.fori_loop(0, block_rows, collect_edges, 0, unroll=8)
    rows_of = fold_lanes(zbuf[...].reshape(block_rows, PH))
    for q in range(4):
        res_flat[0, q : q + 1, :] = local_sum[:, q * PH : (q + 1) * PH] + to_flat_rows(rows_of, q)
    stage_a[1, pl.ds(zc, 1)] = res_flat[...]
    group_copies(lambda step: res_flat, stage_a.at[1], zc, zc_peer, n_zc, a_sem.at[1])
    partial_sums(1)

    arrive(stage_b.at[0], n_xy - 1, b_sem.at[0])
    denominator = jnp.sum(stage_b[0], axis=0)
    arrive(stage_b.at[1], n_xy - 1, b_sem.at[1])
    correction = jnp.sum(stage_b[1], axis=0) / denominator
    eye = iota((PH, PH), 0) == iota((PH, PH), 1)
    for q in range(4):
        column = jnp.sum(jnp.where(eye, correction[q : q + 1, :], 0.0), axis=1, keepdims=True)
        out_ref[q * 8 : (q + 1) * 8] = out_ref[q * 8 : (q + 1) * 8] + column.reshape(8, NV, 1)

    drain(msg, n_rows - 1, req_sem)
    drain(meta_s, n_zc - 1, agg_sem.at[0])
    drain(meta_t, n_xy - 1, agg_sem.at[1])
    for which in range(2):
        for part in range(PARTS):
            drain(send_big.at[which].at[part], 2 * (n_rows - 1), big_sem.at[which].at[part])
            for copy in bands[which][part]:
                copy.wait_send()
        drain(stage_a.at[which], n_zc - 1, a_sem.at[which])
        drain(stage_o.at[which], n_xy - 1, b_sem.at[which])
    drain(recv_small, n_rows - 1, small_sem)
    for copy in uband:
        copy.wait_send()


def on_device(
    start_iterate,
    right_side,
    diag_table,
    inverse_table,
    coupling_tiles,
    diag_index,
    tile_index,
    source_owner,
    source_local,
    aggregate_map,
):
    n_band = lax.axis_size("band")
    n_rows = lax.axis_size("rows")
    block_rows = start_iterate.shape[0]
    n_x, n_z = GRID_XZ[n_rows]
    n_zc, n_xy = n_z * CORES, n_x * n_band
    flat = block_rows * NV
    vmem = pltpu.VMEM
    dma = pltpu.SemaphoreType.DMA
    full = pl.BlockSpec(memory_space=pltpu.VMEM)
    scratch = [
        vmem((block_rows, NV, PH), F32),
        vmem(diag_table.shape, F32),
        vmem(diag_table.shape, F32),
        vmem(diag_table.shape, F32),
        dma((6,)),
        pltpu.SMEM(diag_index.shape, I32),
        pltpu.SMEM(tile_index.shape[::-1], I32),
        pltpu.SMEM(source_owner.shape[::-1], I32),
        pltpu.SMEM(source_local.shape[::-1], I32),
        pltpu.SMEM(aggregate_map.shape[::-1], I32),
        dma((5,)),
        vmem((4 * block_rows, NT, PH), F32),
        vmem((block_rows, NT, PH), F32),
        vmem((NT * PH, 2 * PH), BF16),
        vmem((NT * PH, 2 * PH), BF16),
        vmem((4 * NT, PH), BF16),
        vmem((NT, 1, PH), F32),
        vmem((flat, NT * PH), BF16),
        vmem((flat // 2, PH), F32),
        vmem((n_rows, 1, PH), I32),
        vmem((1, 1, PH), I32),
        pltpu.SMEM((n_rows, 1, PH), I32),
        pltpu.SMEM((1, 1, PH), I32),
        vmem((1, 1, PH), F32),
        vmem((n_zc, 1, PH), F32),
        vmem((n_xy, 1, PH), F32),
        vmem((n_xy * block_rows, n_zc * block_rows), BF16),
        vmem((1, 4, PH), F32),
        vmem((1, 4, PH), F32),
        vmem((2, n_zc, 4, PH), F32),
        vmem((2, n_xy, 4, PH), F32),
        vmem((n_zc * block_rows, PH), F32),
        vmem((n_xy * block_rows, PH), F32),
        vmem((2, n_xy, 4, PH), F32),
        vmem((2, PARTS, 2 * n_rows, HALF, PH), F32),
        vmem((2 * n_rows, HALF, PH), F32),
        vmem((2 * n_rows, HALF, PH), F32),
        vmem((2 * n_rows, HALF, PH), F32),
        vmem((2 * n_rows, HALF, PH), F32),
        vmem((2, PARTS, block_rows, HALF, PH), F32),
        vmem((2, PARTS, block_rows, HALF, PH), F32),
        vmem((block_rows, HALF, PH), F32),
        vmem((block_rows, HALF, PH), F32),
        vmem((block_rows, HALF, PH), F32),
        vmem((block_rows, HALF, PH), F32),
        vmem((2, 2 * n_rows * NV, PH), BF16),
        vmem((n_rows // 4, 1, PH), F32),
        vmem((n_rows, 1, PH), F32),
        vmem((NT, flat), F32),
        vmem((NT, flat), F32),
        vmem((NT, flat), F32),
        vmem((block_rows, 1, PH), F32),
        dma((3,)),
        dma((2, 2)),
        dma((2, PARTS, 2)),
        dma((2, PARTS, 2, 2)),
        dma((2,)),
        dma((2, 2)),
        dma((2, 2)),
        dma((2, 2)),
        dma((2,)),
    ]
    return pl.pallas_call(
        functools.partial(kernel, n_band, n_rows),
        out_shape=jax.ShapeDtypeStruct(start_iterate.shape, F32),
        in_specs=[pl.BlockSpec(memory_space=pl.ANY)] * 10,
        out_specs=full,
        scratch_shapes=scratch,
        compiler_params=pltpu.CompilerParams(
            collective_id=0, has_side_effects=True, vmem_limit_bytes=67043328
        ),
    )(
        diag_index,
        tile_index.T,
        source_owner.T,
        source_local.T,
        aggregate_map.T,
        start_iterate,
        right_side,
        diag_table,
        inverse_table,
        coupling_tiles,
    )


def solution(mesh):
    in_specs = (
        P(("band", "rows"), None, None),
        P(("band", "rows"), None, None),
        P(),
        P(),
        P(),
        P(("band", "rows")),
        P(("band", "rows"), None),
        P(("band", "rows"), None),
        P(("band", "rows"), None),
        P(("band", "rows"), None),
    )
    out_specs = P(("band", "rows"), None, None)
    return jax.shard_map(
        on_device, mesh=mesh, in_specs=in_specs, out_specs=out_specs, check_vma=False
    )
```
